32 devices in a mesh: sect: 4 (over z), dom: 8 (over y, x, core).
Axes of the slice: x: 2, y: 2, z: 4, core: 2. Of those that a mesh axis runs over, the one named last changes fastest.
Arguments:
- state: float32 [2048, 4096], P('sect', 'dom'), may hold values from -6 to 6
- previous: float32 [2048, 4096], P('sect', 'dom'), may hold values from -6 to 6
- coefficient: float32 [2048, 4096], P('sect', 'dom'), may hold values from 0.1 to 0.4
- stiffness: bfloat16 [4, 128, 128], replicated, may hold values from -1 to 1, as said below
- waveform: float32 [8, 32, 512], P(None, ('sect', 'dom')), may hold values from -6 to 6
- entry_face: int32 [1024], P(('sect', 'dom')), may hold values from 0 to 3
- entry_owner: int32 [1024, 1], P(('sect', 'dom')), may hold values from 0 to 7; in each aligned block of 32 rows (0 to 31, 32 to 63, ...) at most 8 rows name the same one
- entry_node: int32 [1024], P(('sect', 'dom')), may hold values from 0 to 3
- rbf: float32 [1024, 128, 128], P(('sect', 'dom')), may hold values from -0.109375 to 0.109375
Outputs:
- state_next: float32 [2048, 4096], P('sect', 'dom')
- previous_next: float32 [2048, 4096], P('sect', 'dom')
- waveform_next: float32 [8, 32, 512], P(None, ('sect', 'dom'))
The draws below stay inside these ranges and needn't reach their ends.
Inputs may be any that keep to these rules, and one draw needn't show every extreme that they name: `entry_owner`: among the entries of one device, at most 8 name the same owner. `stiffness`: each element block is symmetric.
All inputs are finite; a program needn't handle non-finite values.
Results may differ from the reference program's by a relative error of at most 0.0006.
Values sent between devices are 32-bit elements; how exact they have to be, the bound alone decides.
A program may use at most 64 MiB of HBM per device.

```python
import math
import jax
import jax.numpy as jnp
import numpy as np
from jax import lax

ROWS = 512
LANES = 512
SUBSTEPS = 8
BLOCK = 128
ELEM = 128
E_DEV = 32
CAP = 8
BLOCKS = 4
ELEM_BLOCKS = 4
ENTRIES = 1024
FAN = 3072
N_SECT = 4
N_DOM = 8


def draw_stiffness(key, part):
    first_key, second_key = jax.random.split(jax.random.fold_in(key, 17))
    diagonal = jax.random.uniform(first_key, (ELEM_BLOCKS, ELEM), jnp.float32, 0.5, 1.0)
    coupling = jax.random.uniform(second_key, (ELEM_BLOCKS, ELEM, ELEM), jnp.float32, -1.0, 1.0)
    coupling = coupling * (0.6 / ELEM)
    symmetric = 0.5 * (coupling + jnp.swapaxes(coupling, -1, -2))
    identity = jnp.eye(ELEM, dtype=jnp.float32)
    matrix = symmetric * (1.0 - identity) + identity * diagonal[..., None]
    return matrix.astype(jnp.bfloat16)


def place_ends(values, rng, smallest, high):
    longest = values.shape.index(max(values.shape))
    spots = []
    for shift in (0, 1):
        where = [jax.random.randint(jax.random.fold_in(rng, axis), (), 0, length) for axis, length in enumerate(values.shape)]
        where[longest] = (where[longest] + shift) % values.shape[longest]
        spots.append(tuple(where))
    return values.at[spots[0]].set(smallest).at[spots[1]].set(high)


def shard_levels(key, dims, pieces, least, largest):
    def one(dim, parts):
        heights = jax.random.uniform(jax.random.fold_in(jax.random.fold_in(key, 6), dim), (parts,), jnp.float32, least / len(pieces), largest / len(pieces))
        return jnp.repeat(jnp.exp(heights), dims[dim] // parts).reshape((-1,) + (1,) * (len(dims) - dim - 1))

    loudness = one(*pieces[0])
    for cut in pieces[1:]:
        loudness = loudness * one(*cut)
    return loudness


def assign_block(stream_key, own, number, rows, count, top, limit, lean):
    order = jax.random.permutation(stream_key, count)
    packed, usual = load_shares(count, rows * top, limit, lean, True), load_shares(count, rows * top, limit, lean, False)
    places = jnp.arange(count)

    def named(sizes, turn):
        used = int((sizes > 0).sum())
        fixed = max(1, used // 4)
        passed = fixed + (places - fixed + turn * (used - fixed)) % max(1, count - fixed)
        return jnp.zeros((count,), jnp.int32).at[order[jnp.where(places < fixed, places, passed)]].set(jnp.asarray(sizes, jnp.int32))

    sizes = jnp.where(number % 4 == 0, named(packed, number // 4), named(usual, number - number // 4 - 1))
    mixed = jax.random.permutation(jax.random.fold_in(own, 3), count)
    source_of, receiver = mixed[0:count // 2 * 2:2], mixed[1:count // 2 * 2:2]
    room = jnp.minimum(sizes[source_of] - 1, limit - sizes[receiver]) // 2
    room = jnp.where((source_of == order[0]) | (receiver == order[0]) | (sizes[receiver] == 0), 0, jnp.maximum(room, 0))
    passed = jax.random.randint(jax.random.fold_in(own, 4), (count // 2,), 0, 1 << 20) % (room + 1)
    sizes = sizes.at[source_of].add(-passed).at[receiver].add(passed)
    labels = jnp.searchsorted(jnp.cumsum(sizes), jnp.arange(rows * top), side="right").astype(jnp.int32)
    listing = labels.reshape(top, rows).T
    listing = listing[jax.random.permutation(jax.random.fold_in(own, 1), rows)]
    turn = jax.random.randint(jax.random.fold_in(own, 2), (rows, 1), 0, top)
    return jnp.take_along_axis(listing, (jnp.arange(top)[None, :] + turn) % top, axis=1)


def load_shares(amount, total, limit, slope, full):
    weights = [(1 << 20) // math.isqrt(standing ** slope) + 1 for standing in range(1, amount + 1)]
    largest = limit if full else min(limit, max(-(-total // amount), total * weights[0] // sum(weights)))
    least = 1 if total - largest >= amount - 1 else 0
    holding, surplus = [largest] + [least] * (amount - 1), total - largest - least * (amount - 1)
    while surplus > 0:
        candidates = [i for i in range(1, amount) if holding[i] < largest] or [i for i in range(1, amount) if holding[i] < limit]
        pool, remaining = sum([weights[i] for i in candidates]), surplus
        for i in candidates:
            extra = min(limit - holding[i], max(1, remaining * weights[i] // pool), surplus)
            holding[i] = holding[i] + extra
            surplus = surplus - extra
    return np.array(holding)


def gaussian(key, extent, width, reach, cuts=(), kind=jnp.bfloat16):
    level = shard_levels(key, extent, cuts, -0.22, 0.18) if cuts else 1.0
    entries = jax.random.normal(key, extent, jnp.float32) * width * level
    return jnp.minimum(jnp.maximum(entries, -reach), reach).astype(kind)


def setup_inputs(seed: int = 0) -> dict:
    keys = jax.random.split(jax.random.key(seed), 10)
    state = gaussian(keys[0], (N_SECT * ROWS, N_DOM * LANES), 1.0, 6.0, ((0, 4), (1, 8)), jnp.float32)
    previous = gaussian(keys[1], (N_SECT * ROWS, N_DOM * LANES), 1.0, 6.0, ((0, 4), (1, 8)), jnp.float32)
    coefficient = jnp.clip(jnp.exp(math.log(0.4) - 1.3862944 * jax.random.uniform(keys[2], (N_SECT * ROWS, N_DOM * LANES), jnp.float32) ** shard_levels(keys[2], (N_SECT * ROWS, N_DOM * LANES), ((0, 4), (1, 8)), -0.2, 0.2)), 0.1, 0.4)
    stiffness = draw_stiffness(jax.random.fold_in(keys[9], 71), 0)
    waveform = gaussian(keys[4], (SUBSTEPS, N_SECT * N_DOM, LANES), 1.0, 6.0, ((1, 32),), jnp.float32)
    entry_face = place_ends(jax.random.randint(keys[5], (ENTRIES,), 0, BLOCKS), jax.random.fold_in(keys[5], 1), 0, BLOCKS - 1).astype(jnp.int32)
    entry_owner_keys = jax.random.split(jax.random.fold_in(keys[6], 1), ENTRIES // E_DEV)
    entry_owner_turns = jax.random.permutation(jax.random.fold_in(keys[6], 3), ENTRIES // E_DEV)
    entry_owner = jax.vmap(lambda own, number: assign_block(jax.random.fold_in(keys[6], 2), own, number, E_DEV, N_DOM, 1, CAP, 2))(entry_owner_keys, entry_owner_turns).reshape((ENTRIES, 1))
    entry_node = place_ends(jax.random.randint(keys[7], (ENTRIES,), 0, BLOCKS), jax.random.fold_in(keys[7], 1), 0, BLOCKS - 1).astype(jnp.int32)
    rbf = gaussian(keys[8], (ENTRIES, BLOCK, BLOCK), FAN ** -0.5, 0.109375, ((0, 32),), jnp.float32)
    return {"state": state, "previous": previous, "coefficient": coefficient, "stiffness": stiffness, "waveform": waveform, "entry_face": entry_face, "entry_owner": entry_owner, "entry_node": entry_node, "rbf": rbf}


def laplacian(field):
    padded = jnp.pad(field, 1)
    near = padded[:-2, 1:-1] + padded[2:, 1:-1]
    near = near + padded[1:-1, :-2] + padded[1:-1, 2:]
    return near - 4.0 * field


def reference(state, previous, coefficient, stiffness, waveform, entry_face, entry_owner, entry_node, rbf):
    fluid_rows = (N_SECT - 1) * ROWS
    fluid_count = (N_SECT - 1) * N_DOM
    fluid_now, fluid_before = state[:fluid_rows], previous[:fluid_rows]
    shell_now, shell_before = state[fluid_rows:], previous[fluid_rows:]
    fluid_coef, shell_coef = coefficient[:fluid_rows], coefficient[fluid_rows:]
    wet_rows = jnp.arange(N_SECT - 1) * ROWS + ROWS - 1
    matrices = stiffness.astype(jnp.float32)
    face_traces = []
    node_traces = []
    for substep in range(SUBSTEPS):
        fluid_source = jnp.zeros_like(fluid_now).at[wet_rows].set(
            waveform[substep, :fluid_count].reshape(N_SECT - 1, N_DOM * LANES))
        fluid_next = 2.0 * fluid_now - fluid_before + fluid_coef * (laplacian(fluid_now) + fluid_source)
        rounded = lax.optimization_barrier(shell_now.astype(jnp.bfloat16)).astype(jnp.float32)
        element_term = jnp.einsum('bic,bij->bjc', rounded.reshape(ELEM_BLOCKS, ELEM, N_DOM * LANES), matrices,
                                  precision=lax.Precision.HIGHEST).reshape(ROWS, N_DOM * LANES)
        shell_source = jnp.zeros_like(shell_now).at[0].set(waveform[substep, fluid_count:].reshape(N_DOM * LANES))
        shell_next = 2.0 * shell_now - shell_before + shell_coef * (laplacian(shell_now) - element_term + shell_source)
        fluid_before, fluid_now = fluid_now, fluid_next
        shell_before, shell_now = shell_now, shell_next
        face_traces.append(fluid_now[wet_rows].reshape(fluid_count, LANES))
        node_traces.append(shell_now[0].reshape(N_DOM, LANES))
    face_trace = jnp.stack(face_traces)
    node_trace = jnp.stack(node_traces)
    entry_total = fluid_count * E_DEV
    faces = entry_face[:entry_total]
    owners = entry_owner[:entry_total, 0]
    nodes = entry_node[:entry_total]
    weights = rbf[:entry_total]
    device_index = jnp.arange(entry_total, dtype=jnp.int32) // E_DEV
    face_blocks = face_trace.reshape(SUBSTEPS, fluid_count, BLOCKS, BLOCK)
    picked = face_blocks[:, device_index, faces]
    contribution = jnp.einsum('kef,efn->ekn', picked, weights, precision=lax.Precision.HIGHEST)
    node_index = owners * BLOCKS + nodes
    loads = jax.ops.segment_sum(contribution, node_index, N_DOM * BLOCKS)
    loads = loads.reshape(N_DOM, BLOCKS, SUBSTEPS, BLOCK).transpose(2, 0, 1, 3).reshape(SUBSTEPS, N_DOM, LANES)
    node_blocks = node_trace.reshape(SUBSTEPS, N_DOM * BLOCKS, BLOCK)
    fetched = node_blocks[:, node_index]
    face_terms = jnp.einsum('ken,efn->ekf', fetched, weights, precision=lax.Precision.HIGHEST)
    face_index = device_index * BLOCKS + faces
    displacements = jax.ops.segment_sum(face_terms, face_index, fluid_count * BLOCKS)
    displacements = displacements.reshape(fluid_count, BLOCKS, SUBSTEPS, BLOCK).transpose(2, 0, 1, 3).reshape(
        SUBSTEPS, fluid_count, LANES)
    state_next = jnp.concatenate([fluid_now, shell_now], 0)
    previous_next = jnp.concatenate([fluid_before, shell_before], 0)
    waveform_next = jnp.concatenate([displacements, loads], 1)
    return state_next, previous_next, waveform_next
```

```python
import functools

import jax
import jax.numpy as jnp
from jax import lax
from jax.experimental import pallas as pl
from jax.experimental.pallas import tpu as pltpu
from jax.sharding import PartitionSpec as P

HALO = 8
TILE = 128
SUB = 8
F32 = jnp.float32
BF16 = jnp.bfloat16
MESH = pl.DeviceIdType.MESH


def remote(source, target, send, recv, section, column):
    return pltpu.make_async_remote_copy(
        src_ref=source,
        dst_ref=target,
        send_sem=send,
        recv_sem=recv,
        device_id=(section, column),
        device_id_type=MESH,
    )


def split(value):
    high = value.astype(BF16)
    low = (value - high.astype(F32)).astype(BF16)
    return high, low


def iota(shape, axis):
    return lax.broadcasted_iota(jnp.int32, shape, axis)


def window_kernel(
    n_sect, n_dom,
    face, owner, node, state, previous, coefficient, stiffness, wave_ref, rbf,
    state_out, previous_out, loads_out, nodes_out,
    nat, planes, scale, wave_t, wave_g, picks, source, above, below, own_wave,
    weights, w_high, w_low, onehot, trace, outgoing, matrices, element, products, term,
    arrived, total, parts, nodes, shell_trace,
    load_sem, out_sem, send_sem, recv_sem,
    load_send, load_recv, part_send, part_recv, down_send, down_recv, node_send, node_recv,
):
    rows, lanes = state.shape
    substeps = wave_ref.shape[0]
    entries = rbf.shape[0]
    tiles = rows // TILE
    blocks = lanes // TILE
    wide = lanes + 2 * HALO
    groups = wide // SUB
    pad = SUB
    own = pad + HALO
    side = tiles
    s = lax.axis_index("sect")
    d = lax.axis_index("dom")
    shell = n_sect - 1
    on_shell = s == shell
    on_fluid = jnp.logical_not(on_shell)
    both = jnp.logical_and
    has_left = d > 0
    has_right = d < n_dom - 1
    has_up = both(s >= 1, s <= n_sect - 2)
    has_down = s <= n_sect - 3
    barrier = pltpu.get_barrier_semaphore()

    def greet(section, column):
        pl.semaphore_signal(barrier, inc=1, device_id=(section, column), device_id_type=MESH)

    diagonals = (
        (both(has_up, has_left), s - 1, d - 1),
        (both(has_up, has_right), s - 1, d + 1),
        (both(has_down, has_left), s + 1, d - 1),
        (both(has_down, has_right), s + 1, d + 1),
    )
    for has, section, column in ((has_up, s - 1, d), (has_down, s + 1, d)) + diagonals:

        @pl.when(has)
        def _(section=section, column=column):
            greet(section, column)

    @pl.when(on_fluid)
    def _():
        for j in range(1, n_dom):
            greet(s, lax.rem(d + j, n_dom))
        greet(shell, d)

    @pl.when(on_shell)
    def _():
        for t in range(shell):
            greet(t, d)

        @pl.when(has_left)
        def _():
            greet(s, d - 1)

        @pl.when(has_right)
        def _():
            greet(s, d + 1)

    def one(flag):
        return jnp.where(flag, 1, 0).astype(jnp.int32)

    sideways = one(has_left) + one(has_right)
    peers = one(has_up) + one(has_down) + sum(one(route[0]) for route in diagonals)
    peers = peers + jnp.where(on_shell, shell + sideways, n_dom).astype(jnp.int32)

    fields = (state, previous, coefficient)
    order = [0, blocks - 1] + list(range(1, blocks - 1))
    loads = {}
    for cb in order:
        for a in range(3):
            copy = pltpu.make_async_copy(
                fields[a].at[:, pl.ds(cb * TILE, TILE)], nat.at[a, cb],
                load_sem.at[a * blocks + cb],
            )
            copy.start()
            loads[a, cb] = copy
    elements = pltpu.make_async_copy(stiffness, matrices, load_sem.at[3 * blocks])
    elements.start()
    maps = pltpu.make_async_copy(rbf, weights, load_sem.at[3 * blocks + 1])
    maps.start()

    last_rows = pl.ds(rows - HALO, HALO)
    for cb in range(blocks):
        piece = jnp.concatenate(
            [wave_ref[k, :, cb * TILE : (cb + 1) * TILE] for k in range(substeps)], 0
        )
        nat[3, cb, last_rows, :] = piece
        own_wave[1 + cb] = piece

    def turn(a, cb):
        loads[a, cb].wait()
        for t in range(tiles):
            block = jnp.concatenate(
                [nat[a, cb, pl.ds(t + 4 * SUB * m, SUB, stride=tiles), :]
                 for m in range(TILE // SUB)], 0,
            )
            planes[a, t, pl.ds(own + cb * TILE, TILE), :] = block.T

    for cb in order[:2]:
        for a in range(3):
            turn(a, cb)

    def columns(start):
        return planes.at[:, pl.ds(0, tiles), pl.ds(start, HALO), :]

    first_rows = pl.ds(0, HALO)
    three = pl.ds(0, 3)
    middle = pl.ds(1, blocks)
    end = blocks - 1
    routes = (
        (has_left, s, d - 1, columns(own), columns(own + lanes),
         has_right, columns(own + lanes)),
        (has_right, s, d + 1, columns(own + lanes - HALO), columns(pad), has_left, columns(pad)),
        (has_up, s - 1, d, nat.at[three, :, first_rows, :], below.at[:, middle],
         has_down, below.at[:, middle]),
        (has_down, s + 1, d, nat.at[:, :, last_rows, :], above.at[:, middle],
         has_up, above.at[:, middle]),
        (diagonals[0][0], s - 1, d - 1, nat.at[three, 0, first_rows, :], below.at[:, blocks + 1],
         both(has_down, has_right), below.at[:, blocks + 1]),
        (diagonals[1][0], s - 1, d + 1, nat.at[three, end, first_rows, :], below.at[:, 0],
         both(has_down, has_left), below.at[:, 0]),
        (diagonals[2][0], s + 1, d - 1, nat.at[:, 0, last_rows, :], above.at[:, blocks + 1],
         both(has_up, has_right), above.at[:, blocks + 1]),
        (diagonals[3][0], s + 1, d + 1, nat.at[:, end, last_rows, :], above.at[:, 0],
         both(has_up, has_left), above.at[:, 0]),
        (has_left, s, d - 1, nat.at[3, 0, last_rows, :], own_wave.at[blocks + 1],
         has_right, own_wave.at[blocks + 1]),
        (has_right, s, d + 1, nat.at[3, end, last_rows, :], own_wave.at[0],
         has_left, own_wave.at[0]),
    )

    for cb in order[2:]:
        for a in range(3):
            loads[a, cb].wait()
    pl.semaphore_wait(barrier, peers)
    copies = []
    for i, (has, section, column, source_ref, target_ref, _, _) in enumerate(routes):
        copy = remote(source_ref, target_ref, send_sem.at[i], recv_sem.at[i], section, column)
        copies.append(copy)

        @pl.when(has)
        def _(copy=copy):
            copy.start()

    def turn_late(a, cb):
        for t in range(tiles):
            block = jnp.concatenate(
                [nat[a, cb, pl.ds(t + 4 * SUB * m, SUB, stride=tiles), :]
                 for m in range(TILE // SUB)], 0,
            )
            planes[a, t, pl.ds(own + cb * TILE, TILE), :] = block.T

    for cb in order[2:]:
        for a in range(3):
            turn_late(a, cb)

    def prepare(t, start, count):
        part = pl.ds(start, count)
        scale[t, part, :] = 2.0 - 4.0 * planes[2, t, part, :]

    for t in range(tiles):
        prepare(t, own, lanes)

    at_own = jnp.where(on_shell, 0, TILE - 1).astype(jnp.int32)
    lane = iota((TILE, 2 * TILE), 0)
    goal = iota((TILE, 2 * TILE), 1)
    for k in range(substeps):
        mine = jnp.logical_or(lane == 40 + k, lane == 56 + k)
        upper = jnp.logical_or(lane == 48 + k, lane == 64 + k)
        hit = jnp.logical_or(both(mine, goal == at_own), both(upper, goal == 2 * TILE - 1))
        picks[k] = jnp.where(hit, 1.0, 0.0).astype(BF16)

    elements.wait()

    @pl.when(on_shell)
    def _():
        width = TILE // tiles
        for b in range(tiles):
            i = iota((TILE, rows), 0)
            n = iota((TILE, rows), 1)
            place = lax.rem(i, tiles) * TILE + width * b + i // tiles
            spread = jnp.where(n == place, 1.0, 0.0).astype(BF16)
            wide_rows = jnp.dot(matrices[b], spread, preferred_element_type=F32)
            for t in range(tiles):
                products[t] = wide_rows[:, t * TILE : (t + 1) * TILE]
            for t in range(tiles):
                for u in range(tiles):
                    element[pl.ds(t * TILE + width * b, width), pl.ds(u * TILE, TILE)] = products[
                        u, pl.ds(t, width, stride=tiles), :
                    ].astype(BF16)

    maps.wait()

    @pl.when(on_fluid)
    def _():
        lanes_e = iota((SUB, entries * SUB), 1)
        goal = jnp.zeros((SUB, entries * SUB), jnp.int32)
        for e in range(entries):
            slot = owner[e] * blocks + node[e]
            goal = jnp.where(lanes_e // SUB == e, slot, goal)
        goal = goal * SUB + lax.rem(lanes_e, SUB)
        size = n_dom * blocks * SUB
        for r in range(0, size, TILE):
            here = iota((TILE, entries * SUB), 0) + r
            onehot[pl.ds(r, TILE), :] = jnp.where(here == goal[0:1, :], 1.0, 0.0).astype(BF16)
        for e in range(entries):
            high, low = split(weights[e])
            w_high[e] = high
            w_low[e] = low

    for i, (_, _, _, _, _, comes, buf) in enumerate(routes):

        @pl.when(comes)
        def _(copy=copies[i]):
            copy.wait_recv()

        @pl.when(jnp.logical_not(comes))
        def _(buf=buf):
            buf[...] = jnp.zeros(buf.shape, F32)

    for t in range(tiles):
        prepare(t, pad, HALO)
        prepare(t, own + lanes, HALO)

    edge = iota((HALO, TILE), 1)
    empty = jnp.zeros((TILE - 8 * HALO, TILE), F32)

    def joined(ref):
        if ref[1] is not None:
            right, left = ref[0][ref[1], blocks + 1], ref[0][ref[1], 0]
        else:
            right, left = ref[0][blocks + 1], ref[0][0]
        return jnp.where(edge < HALO, right, jnp.where(edge >= TILE - HALO, left, 0.0))

    def straight(q):
        def pick(ref):
            return ref[0][ref[1], q] if ref[1] is not None else ref[0][q]

        return pick

    def stacked(pick):
        parts_list = [
            pick((below, 0)), pick((above, 1)), pick((below, 1)), pick((above, 2)),
            pick((below, 2)), pick((own_wave, None)), pick((above, 3)), empty, pick((above, 0)),
        ]
        return jnp.concatenate(parts_list, 0).T

    def lay(block, start, count, base):
        part = pl.ds(start, count)
        cut = block[base : base + count]
        planes[0, side, part, :] = cut
        planes[1, side, part, :] = pltpu.roll(cut, TILE - 2 * HALO, 1)
        coef = pltpu.roll(cut, TILE - 4 * HALO, 1)
        planes[2, side, part, :] = coef
        scale[side, part, :] = 2.0 - 4.0 * coef
        at = iota((count, TILE), 1)
        keep = both(at >= 5 * HALO, at < 7 * HALO)
        wave_t[part, :] = jnp.where(keep, cut, 0.0)

    for q in range(blocks):
        lay(stacked(straight(1 + q)), own + q * TILE, TILE, 0)
    corner = stacked(joined)
    lay(corner, own + lanes, HALO, 0)
    lay(corner, pad, HALO, TILE - HALO)

    for g in range(0, groups, 2):
        pair = jnp.concatenate(
            [wave_t[pl.ds(pad + g + i, SUB, stride=groups), :] for i in range(2)], 0
        )
        high = pair.astype(BF16).astype(F32)
        low = pltpu.roll(pair - high, 2 * HALO, 1)
        wave_g[pl.ds(g * SUB, 2 * SUB), :] = (high + low).astype(BF16)

    for i, route in enumerate(routes):

        @pl.when(route[0])
        def _(copy=copies[i]):
            copy.wait_send()

    lane8 = iota((SUB, TILE), 1)
    is_first = lane8 == 0
    is_last = lane8 == TILE - 1

    def row_of(count, g):
        return (pl.ds(0, count), pl.ds(pad + g, SUB, stride=groups), slice(None))

    def note(k, target, tile, row):
        for cb in range(blocks):
            block = planes[target, tile, pl.ds(own + cb * TILE, TILE), :].T
            trace[cb, pl.ds(k, 1), :] = block[row : row + 1]

    def fluid_step(k, cur, other):
        source[...] = jnp.dot(wave_g[...], picks[k], preferred_element_type=F32)
        count = tiles + 1
        now, old, coef = planes.at[cur], planes.at[other], planes.at[2]
        prev, here = now[row_of(count, -1)], now[row_of(count, 0)]
        for g in range(groups):
            after = now[row_of(count, g + 1)]
            side_up, side_down = pltpu.roll(here[side], 1, 1), pltpu.roll(here[side], TILE - 1, 1)
            tail, head = pltpu.roll(here[tiles - 1], 1, 1), pltpu.roll(here[0], TILE - 1, 1)
            up = jnp.concatenate(
                [jnp.where(is_first, side_up, tail)[None], here[: tiles - 1],
                 jnp.where(is_first, tail, side_up)[None]], 0)
            part = slice(g * SUB, (g + 1) * SUB)
            down = jnp.concatenate(
                [here[1:tiles],
                 (jnp.where(is_last, side_down, head) + source[part, :TILE])[None],
                 (jnp.where(is_last, head, side_down) + source[part, TILE:])[None]], 0)
            near = (prev + after) + (up + down)
            at = row_of(count, g)
            old[at] = (scale[at] * here - old[at]) + coef[at] * near
            prev, here = here, after
        note(k, other, tiles - 1, TILE - 1)

    def shell_step(k, cur, other):
        inner = pl.ds(pad, wide)
        rounded = jnp.concatenate(
            [planes[cur, t, inner, :].astype(BF16) for t in range(tiles)], 1
        )
        result = jnp.dot(rounded, element[...], preferred_element_type=F32)
        for t in range(tiles):
            term[t, inner, :] = result[:, t * TILE : (t + 1) * TILE]
        source[:, :TILE] = jnp.dot(
            wave_g[...], picks[k, :, :TILE], preferred_element_type=F32
        )
        count = tiles
        now, old, coef = planes.at[cur], planes.at[other], planes.at[2]
        prev, here = now[row_of(count, -1)], now[row_of(count, 0)]
        for g in range(groups):
            after = now[row_of(count, g + 1)]
            tail, head = pltpu.roll(here[tiles - 1], 1, 1), pltpu.roll(here[0], TILE - 1, 1)
            part = slice(g * SUB, (g + 1) * SUB)
            up = jnp.concatenate(
                [(jnp.where(is_first, 0.0, tail) + source[part, :TILE])[None],
                 here[: tiles - 1]], 0)
            down = jnp.concatenate([here[1:tiles], jnp.where(is_last, 0.0, head)[None]], 0)
            at = row_of(count, g)
            near = (prev + after) + (up + down) - term[at]
            old[at] = (scale[at] * here - old[at]) + coef[at] * near
            prev, here = here, after
        note(k, other, 0, 0)

    def pair_of(step):
        def body(i, carry):
            step(2 * i, 0, 1)
            step(2 * i + 1, 1, 0)
            return carry

        lax.fori_loop(0, substeps // 2, body, 0)

    for ref in (planes.at[0], planes.at[1]):
        for t in range(tiles + 1):
            ref[t, pl.ds(0, pad), :] = jnp.zeros((pad, TILE), F32)
            ref[t, pl.ds(pad + wide, pad), :] = jnp.zeros((pad, TILE), F32)

    def hand_out():
        leave = []
        for a, target in ((0, state_out), (1, previous_out)):
            for cb in range(blocks):
                for t in range(tiles):
                    block = planes[a, t, pl.ds(own + cb * TILE, TILE), :].T
                    for m in range(TILE // SUB):
                        nat[a, cb, pl.ds(t + 4 * SUB * m, SUB, stride=tiles), :] = block[
                            m * SUB : (m + 1) * SUB
                        ]
                copy = pltpu.make_async_copy(
                    nat.at[a, cb], target.at[:, pl.ds(cb * TILE, TILE)],
                    out_sem.at[a * blocks + cb],
                )
                copy.start()
                leave.append(copy)
        return leave

    @pl.when(on_shell)
    def _():
        pair_of(shell_step)
        sends = []
        for t in range(shell):
            copy = remote(trace, shell_trace, down_send.at[t], down_recv, t, d)
            copy.start()
            sends.append(copy)
        nodes_out[...] = jnp.zeros_like(nodes_out)
        leave = hand_out()
        for t in range(shell):
            remote(total, parts.at[t], part_send, part_recv.at[t], t, d).wait_recv()
        sums = parts[0]
        for t in range(1, shell):
            sums = sums + parts[t]
        loads_out[...] = sums
        for copy in sends:
            copy.wait_send()
        for copy in leave:
            copy.wait()

    @pl.when(on_fluid)
    def _():
        pair_of(fluid_step)
        terms = []
        for e in range(entries):
            x_high, x_low = split(trace[face[e]])
            first = jnp.dot(
                jnp.concatenate([x_high, x_low], 0), w_high[e], preferred_element_type=F32
            )
            second = jnp.dot(x_high, w_low[e], preferred_element_type=F32)
            terms.append(first[:SUB] + first[SUB:] + second)
        high, low = split(jnp.concatenate(terms, 0))
        halves = jnp.concatenate([high, low], 1)
        size = blocks * SUB
        for o in range(0, n_dom * size, TILE):
            result = jnp.dot(onehot[pl.ds(o, TILE), :], halves, preferred_element_type=F32)
            result = result[:, :TILE] + result[:, TILE:]
            for j in range(TILE // size):
                for b in range(blocks):
                    at = j * size + b * SUB
                    outgoing[o // size + j, b] = result[at : at + SUB]
        sends = []
        for j in range(1, n_dom):
            to = lax.rem(d + j, n_dom)
            copy = remote(
                outgoing.at[to], arrived.at[j - 1], load_send.at[j - 1], load_recv.at[j - 1],
                s, to,
            )
            copy.start()
            sends.append(copy)
        remote(trace, shell_trace, down_send.at[0], down_recv, shell, d).wait_recv()
        spread = []
        for j in range(1, n_dom):
            to = lax.rem(d + j, n_dom)
            copy = remote(
                shell_trace, nodes.at[j - 1], node_send.at[j - 1], node_recv.at[j - 1], s, to
            )
            copy.start()
            spread.append(copy)
        leave = hand_out()
        value = outgoing[d]
        for j in range(1, n_dom):
            sends[j - 1].wait_recv()
            value = value + arrived[j - 1]
        total[...] = value
        up = remote(total, parts.at[s], part_send, part_recv.at[s], shell, d)
        up.start()
        loads_out[...] = jnp.zeros_like(loads_out)
        nodes_out[0] = shell_trace[...]
        for j in range(1, n_dom):
            spread[j - 1].wait_recv()
            nodes_out[j] = nodes[j - 1]
        for copy in sends + spread + [up]:
            copy.wait_send()
        for copy in leave:
            copy.wait()


def window(
    face, owner, node, state, previous, coefficient, stiffness, wave, rbf, n_sect, n_dom
):
    rows, lanes = state.shape
    substeps = wave.shape[0]
    entries, size = rbf.shape[0], rbf.shape[1]
    tiles, blocks = rows // TILE, lanes // TILE
    wide = lanes + 2 * HALO
    deep = wide + 2 * SUB
    smem = pl.BlockSpec(memory_space=pltpu.SMEM)
    anywhere = pl.BlockSpec(memory_space=pl.ANY)
    vmem = pl.BlockSpec(memory_space=pltpu.VMEM)
    dma = pltpu.SemaphoreType.DMA
    block = (blocks, substeps, size)

    def full(*shape, dtype=F32):
        return pltpu.VMEM(shape, dtype)

    return pl.pallas_call(
        functools.partial(window_kernel, n_sect, n_dom),
        out_shape=(
            jax.ShapeDtypeStruct((rows, lanes), F32),
            jax.ShapeDtypeStruct((rows, lanes), F32),
            jax.ShapeDtypeStruct(block, F32),
            jax.ShapeDtypeStruct((n_dom,) + block, F32),
        ),
        in_specs=[smem] * 3 + [anywhere] * 4 + [vmem] + [anywhere],
        out_specs=(anywhere, anywhere, vmem, vmem),
        scratch_shapes=[
            full(4, blocks, rows, TILE),
            full(3, tiles + 1, deep, TILE),
            full(tiles + 1, deep, TILE),
            full(deep, TILE),
            full(wide, TILE, dtype=BF16),
            full(substeps, TILE, 2 * TILE, dtype=BF16),
            full(wide, 2 * TILE),
            full(4, blocks + 2, HALO, TILE),
            full(3, blocks + 2, HALO, TILE),
            full(blocks + 2, HALO, TILE),
            full(*rbf.shape),
            full(*rbf.shape, dtype=BF16),
            full(*rbf.shape, dtype=BF16),
            full(n_dom * blocks * SUB, entries * SUB, dtype=BF16),
            full(*block),
            full(n_dom, *block),
            full(*stiffness.shape, dtype=BF16),
            full(rows, rows, dtype=BF16),
            full(tiles, TILE, TILE),
            full(tiles, deep, TILE),
            full(n_dom - 1, *block),
            full(*block),
            full(n_sect - 1, *block),
            full(n_dom - 1, *block),
            full(*block),
            dma((3 * blocks + 2,)),
            dma((2 * blocks,)),
            dma((10,)),
            dma((10,)),
            dma((n_dom - 1,)),
            dma((n_dom - 1,)),
            dma,
            dma((n_sect - 1,)),
            dma((n_sect - 1,)),
            dma,
            dma((n_dom - 1,)),
            dma((n_dom - 1,)),
        ],
        compiler_params=pltpu.CompilerParams(
            collective_id=0, has_side_effects=True, vmem_limit_bytes=40 * 1024 * 1024
        ),
        name="window",
    )(face, owner, node, state, previous, coefficient, stiffness, wave, rbf)


def three_products(x, high, low):
    x_high, x_low = split(x)
    dims = (((1,), (1,)), ((), ()))
    both = jnp.concatenate([x_high, x_low], 0)
    first = lax.dot_general(both, high, dims, preferred_element_type=F32)
    second = lax.dot_general(x_high, low, dims, preferred_element_type=F32)
    return first[:SUB] + first[SUB:] + second


def pull_kernel(
    n_sect, n_dom, face, owner, node, state, previous, loads, nodes, rbf,
    state_out, previous_out, out, weights, terms, sums, sems,
):
    entries = rbf.shape[0]
    substeps = out.shape[0]
    blocks = loads.shape[0]
    d = lax.axis_index("dom")
    on_shell = lax.axis_index("sect") == n_sect - 1
    maps = pltpu.make_async_copy(rbf, weights, sems.at[0])
    leave = [
        pltpu.make_async_copy(state, state_out, sems.at[1]),
        pltpu.make_async_copy(previous, previous_out, sems.at[2]),
    ]

    @pl.when(jnp.logical_not(on_shell))
    def _():
        maps.start()

    for copy in leave:
        copy.start()

    @pl.when(on_shell)
    def _():
        for b in range(blocks):
            for k in range(substeps):
                out[k, :, b * TILE : (b + 1) * TILE] = loads[b, k : k + 1, :]

    @pl.when(jnp.logical_not(on_shell))
    def _():
        sums[...] = jnp.zeros_like(sums)
        maps.wait()
        for e in range(entries):
            slot = lax.rem(d - owner[e] + n_dom, n_dom)
            high, low = split(weights[e])
            terms[e] = three_products(nodes[slot, node[e]], high, low)
        for e in range(entries):
            sums[face[e]] += terms[e]
        for b in range(blocks):
            for k in range(substeps):
                out[k, :, b * TILE : (b + 1) * TILE] = sums[b, k : k + 1, :]

    for copy in leave:
        copy.wait()


def pull(face, owner, node, state, previous, loads, nodes, rbf, n_sect, n_dom):
    blocks, substeps, size = loads.shape
    smem = pl.BlockSpec(memory_space=pltpu.SMEM)
    anywhere = pl.BlockSpec(memory_space=pl.ANY)
    vmem = pl.BlockSpec(memory_space=pltpu.VMEM)
    return pl.pallas_call(
        functools.partial(pull_kernel, n_sect, n_dom),
        out_shape=(
            jax.ShapeDtypeStruct(state.shape, F32),
            jax.ShapeDtypeStruct(state.shape, F32),
            jax.ShapeDtypeStruct((substeps, 1, blocks * size), F32),
        ),
        in_specs=[smem] * 3 + [anywhere] * 2 + [vmem] * 2 + [anywhere],
        out_specs=(anywhere, anywhere, vmem),
        scratch_shapes=[
            pltpu.VMEM(rbf.shape, F32),
            pltpu.VMEM((rbf.shape[0], substeps, size), F32),
            pltpu.VMEM((blocks, substeps, size), F32),
            pltpu.SemaphoreType.DMA((3,)),
        ],
        compiler_params=pltpu.CompilerParams(vmem_limit_bytes=24 * 1024 * 1024),
        name="pull",
    )(face, owner, node, state, previous, loads, nodes, rbf)


def local(
    state, previous, coefficient, stiffness, waveform, entry_face, entry_owner, entry_node, rbf
):
    n_sect = lax.axis_size("sect")
    n_dom = lax.axis_size("dom")
    owner = entry_owner.reshape(entry_owner.shape[0])
    current, before, loads, nodes = window(
        entry_face, owner, entry_node, state, previous, coefficient, stiffness, waveform, rbf,
        n_sect, n_dom,
    )
    return pull(
        entry_face, owner, entry_node, current, before, loads, nodes, rbf, n_sect, n_dom
    )


def solution(mesh):
    in_specs = (
        P("sect", "dom"),
        P("sect", "dom"),
        P("sect", "dom"),
        P(),
        P(None, ("sect", "dom"), None),
        P(("sect", "dom")),
        P(("sect", "dom"), None),
        P(("sect", "dom")),
        P(("sect", "dom"), None, None),
    )
    out_specs = (P("sect", "dom"), P("sect", "dom"), P(None, ("sect", "dom"), None))
    return jax.shard_map(local, mesh=mesh, in_specs=in_specs, out_specs=out_specs, check_vma=False)
```

```python
import functools

import jax
import jax.numpy as jnp
from jax import lax
from jax.experimental import pallas as pl
from jax.experimental.pallas import tpu as pltpu
from jax.sharding import PartitionSpec as P

HALO = 8
TILE = 128
SUB = 8
F32 = jnp.float32
BF16 = jnp.bfloat16
MESH = pl.DeviceIdType.MESH
PARTS = 4


def remote(source, target, send, recv, section, column):
    return pltpu.make_async_remote_copy(
        src_ref=source,
        dst_ref=target,
        send_sem=send,
        recv_sem=recv,
        device_id=(section, column),
        device_id_type=MESH,
    )


def split(value):
    high = value.astype(BF16)
    low = (value - high.astype(F32)).astype(BF16)
    return high, low


def iota(shape, axis):
    return lax.broadcasted_iota(jnp.int32, shape, axis)


def window_kernel(
    n_sect, n_dom,
    face, owner, node, state, previous, coefficient, stiffness, wave_ref, rbf,
    state_out, previous_out, loads_out, nodes_out,
    nat, planes, scale, wave_t, wave_g, picks, source, above, below, own_wave,
    weights, w_high, w_low, onehot, trace, outgoing, matrices, element, products, term,
    arrived, total, parts, nodes, shell_trace,
    load_sem, out_sem, send_sem, recv_sem,
    load_send, load_recv, part_send, part_recv, down_send, down_recv, node_send, node_recv,
):
    rows, lanes = state.shape
    substeps = wave_ref.shape[0]
    entries = rbf.shape[0]
    tiles = rows // TILE
    blocks = lanes // TILE
    wide = lanes + 2 * HALO
    groups = wide // SUB
    pad = SUB
    own = pad + HALO
    side = tiles
    s = lax.axis_index("sect")
    d = lax.axis_index("dom")
    shell = n_sect - 1
    on_shell = s == shell
    on_fluid = jnp.logical_not(on_shell)
    both = jnp.logical_and
    has_left = d > 0
    has_right = d < n_dom - 1
    has_up = both(s >= 1, s <= n_sect - 2)
    has_down = s <= n_sect - 3
    barrier = pltpu.get_barrier_semaphore()

    def greet(section, column):
        pl.semaphore_signal(barrier, inc=1, device_id=(section, column), device_id_type=MESH)

    diagonals = (
        (both(has_up, has_left), s - 1, d - 1),
        (both(has_up, has_right), s - 1, d + 1),
        (both(has_down, has_left), s + 1, d - 1),
        (both(has_down, has_right), s + 1, d + 1),
    )
    for has, section, column in ((has_up, s - 1, d), (has_down, s + 1, d)) + diagonals:

        @pl.when(has)
        def _(section=section, column=column):
            greet(section, column)

    @pl.when(on_fluid)
    def _():
        for j in range(1, n_dom):
            greet(s, lax.rem(d + j, n_dom))
        greet(shell, d)

    @pl.when(on_shell)
    def _():
        for t in range(shell):
            greet(t, d)

        @pl.when(has_left)
        def _():
            greet(s, d - 1)

        @pl.when(has_right)
        def _():
            greet(s, d + 1)

    def one(flag):
        return jnp.where(flag, 1, 0).astype(jnp.int32)

    sideways = one(has_left) + one(has_right)
    peers = one(has_up) + one(has_down) + sum(one(route[0]) for route in diagonals)
    peers = peers + jnp.where(on_shell, shell + sideways, n_dom).astype(jnp.int32)

    fields = (state, previous, coefficient)
    order = [0, blocks - 1] + list(range(1, blocks - 1))
    loads = {}
    for cb in order:
        for a in range(3):
            copy = pltpu.make_async_copy(
                fields[a].at[:, pl.ds(cb * TILE, TILE)], nat.at[a, cb],
                load_sem.at[a * blocks + cb],
            )
            copy.start()
            loads[a, cb] = copy
    elements = pltpu.make_async_copy(stiffness, matrices, load_sem.at[3 * blocks])
    elements.start()
    maps = pltpu.make_async_copy(rbf, weights, load_sem.at[3 * blocks + 1])
    maps.start()

    last_rows = pl.ds(rows - HALO, HALO)
    for cb in range(blocks):
        piece = jnp.concatenate(
            [wave_ref[k, :, cb * TILE : (cb + 1) * TILE] for k in range(substeps)], 0
        )
        nat[3, cb, last_rows, :] = piece
        own_wave[1 + cb] = piece

    def turn(a, cb):
        loads[a, cb].wait()
        for t in range(tiles):
            block = jnp.concatenate(
                [nat[a, cb, pl.ds(t + 4 * SUB * m, SUB, stride=tiles), :]
                 for m in range(TILE // SUB)], 0,
            )
            planes[a, t, pl.ds(own + cb * TILE, TILE), :] = block.T

    for cb in order[:2]:
        for a in range(3):
            turn(a, cb)

    def columns(start):
        return planes.at[:, pl.ds(0, tiles), pl.ds(start, HALO), :]

    first_rows = pl.ds(0, HALO)
    three = pl.ds(0, 3)
    middle = pl.ds(1, blocks)
    end = blocks - 1
    routes = (
        (has_left, s, d - 1, columns(own), columns(own + lanes),
         has_right, columns(own + lanes)),
        (has_right, s, d + 1, columns(own + lanes - HALO), columns(pad), has_left, columns(pad)),
        (has_up, s - 1, d, nat.at[three, :, first_rows, :], below.at[:, middle],
         has_down, below.at[:, middle]),
        (has_down, s + 1, d, nat.at[:, :, last_rows, :], above.at[:, middle],
         has_up, above.at[:, middle]),
        (diagonals[0][0], s - 1, d - 1, nat.at[three, 0, first_rows, :], below.at[:, blocks + 1],
         both(has_down, has_right), below.at[:, blocks + 1]),
        (diagonals[1][0], s - 1, d + 1, nat.at[three, end, first_rows, :], below.at[:, 0],
         both(has_down, has_left), below.at[:, 0]),
        (diagonals[2][0], s + 1, d - 1, nat.at[:, 0, last_rows, :], above.at[:, blocks + 1],
         both(has_up, has_right), above.at[:, blocks + 1]),
        (diagonals[3][0], s + 1, d + 1, nat.at[:, end, last_rows, :], above.at[:, 0],
         both(has_up, has_left), above.at[:, 0]),
        (has_left, s, d - 1, nat.at[3, 0, last_rows, :], own_wave.at[blocks + 1],
         has_right, own_wave.at[blocks + 1]),
        (has_right, s, d + 1, nat.at[3, end, last_rows, :], own_wave.at[0],
         has_left, own_wave.at[0]),
    )

    for cb in order[2:]:
        for a in range(3):
            loads[a, cb].wait()
    pl.semaphore_wait(barrier, peers)
    copies = []
    for i, (has, section, column, source_ref, target_ref, _, _) in enumerate(routes):
        copy = remote(source_ref, target_ref, send_sem.at[i], recv_sem.at[i], section, column)
        copies.append(copy)

        @pl.when(has)
        def _(copy=copy):
            copy.start()

    def turn_late(a, cb):
        for t in range(tiles):
            block = jnp.concatenate(
                [nat[a, cb, pl.ds(t + 4 * SUB * m, SUB, stride=tiles), :]
                 for m in range(TILE // SUB)], 0,
            )
            planes[a, t, pl.ds(own + cb * TILE, TILE), :] = block.T

    for cb in order[2:]:
        for a in range(3):
            turn_late(a, cb)

    def prepare(t, start, count):
        part = pl.ds(start, count)
        scale[t, part, :] = 2.0 - 4.0 * planes[2, t, part, :]

    for t in range(tiles):
        prepare(t, own, lanes)

    at_own = jnp.where(on_shell, 0, TILE - 1).astype(jnp.int32)
    lane = iota((TILE, 2 * TILE), 0)
    goal = iota((TILE, 2 * TILE), 1)
    for k in range(substeps):
        mine = jnp.logical_or(lane == 40 + k, lane == 56 + k)
        upper = jnp.logical_or(lane == 48 + k, lane == 64 + k)
        hit = jnp.logical_or(both(mine, goal == at_own), both(upper, goal == 2 * TILE - 1))
        picks[k] = jnp.where(hit, 1.0, 0.0).astype(BF16)

    elements.wait()

    @pl.when(on_shell)
    def _():
        width = TILE // tiles
        for b in range(tiles):
            i = iota((TILE, rows), 0)
            n = iota((TILE, rows), 1)
            place = lax.rem(i, tiles) * TILE + width * b + i // tiles
            spread = jnp.where(n == place, 1.0, 0.0).astype(BF16)
            wide_rows = jnp.dot(matrices[b], spread, preferred_element_type=F32)
            for t in range(tiles):
                products[t] = wide_rows[:, t * TILE : (t + 1) * TILE]
            for t in range(tiles):
                for u in range(tiles):
                    element[pl.ds(t * TILE + width * b, width), pl.ds(u * TILE, TILE)] = products[
                        u, pl.ds(t, width, stride=tiles), :
                    ].astype(BF16)

    maps.wait()

    @pl.when(on_fluid)
    def _():
        lanes_e = iota((SUB, entries * SUB), 1)
        goal = jnp.zeros((SUB, entries * SUB), jnp.int32)
        for e in range(entries):
            slot = owner[e] * blocks + node[e]
            goal = jnp.where(lanes_e // SUB == e, slot, goal)
        goal = goal * SUB + lax.rem(lanes_e, SUB)
        size = n_dom * blocks * SUB
        for r in range(0, size, TILE):
            here = iota((TILE, entries * SUB), 0) + r
            onehot[pl.ds(r, TILE), :] = jnp.where(here == goal[0:1, :], 1.0, 0.0).astype(BF16)
        for e in range(entries):
            high, low = split(weights[e])
            w_high[e] = high
            w_low[e] = low

    for i, (_, _, _, _, _, comes, buf) in enumerate(routes):

        @pl.when(comes)
        def _(copy=copies[i]):
            copy.wait_recv()

        @pl.when(jnp.logical_not(comes))
        def _(buf=buf):
            buf[...] = jnp.zeros(buf.shape, F32)

    for t in range(tiles):
        prepare(t, pad, HALO)
        prepare(t, own + lanes, HALO)

    edge = iota((HALO, TILE), 1)
    empty = jnp.zeros((TILE - 8 * HALO, TILE), F32)

    def joined(ref):
        if ref[1] is not None:
            right, left = ref[0][ref[1], blocks + 1], ref[0][ref[1], 0]
        else:
            right, left = ref[0][blocks + 1], ref[0][0]
        return jnp.where(edge < HALO, right, jnp.where(edge >= TILE - HALO, left, 0.0))

    def straight(q):
        def pick(ref):
            return ref[0][ref[1], q] if ref[1] is not None else ref[0][q]

        return pick

    def stacked(pick):
        parts_list = [
            pick((below, 0)), pick((above, 1)), pick((below, 1)), pick((above, 2)),
            pick((below, 2)), pick((own_wave, None)), pick((above, 3)), empty, pick((above, 0)),
        ]
        return jnp.concatenate(parts_list, 0).T

    def lay(block, start, count, base):
        part = pl.ds(start, count)
        cut = block[base : base + count]
        planes[0, side, part, :] = cut
        planes[1, side, part, :] = pltpu.roll(cut, TILE - 2 * HALO, 1)
        coef = pltpu.roll(cut, TILE - 4 * HALO, 1)
        planes[2, side, part, :] = coef
        scale[side, part, :] = 2.0 - 4.0 * coef
        at = iota((count, TILE), 1)
        keep = both(at >= 5 * HALO, at < 7 * HALO)
        wave_t[part, :] = jnp.where(keep, cut, 0.0)

    for q in range(blocks):
        lay(stacked(straight(1 + q)), own + q * TILE, TILE, 0)
    corner = stacked(joined)
    lay(corner, own + lanes, HALO, 0)
    lay(corner, pad, HALO, TILE - HALO)

    for g in range(0, groups, 2):
        pair = jnp.concatenate(
            [wave_t[pl.ds(pad + g + i, SUB, stride=groups), :] for i in range(2)], 0
        )
        high = pair.astype(BF16).astype(F32)
        low = pltpu.roll(pair - high, 2 * HALO, 1)
        wave_g[pl.ds(g * SUB, 2 * SUB), :] = (high + low).astype(BF16)

    for i, route in enumerate(routes):

        @pl.when(route[0])
        def _(copy=copies[i]):
            copy.wait_send()

    lane8 = iota((SUB, TILE), 1)
    is_first = lane8 == 0
    is_last = lane8 == TILE - 1

    def row_of(count, g):
        return (pl.ds(0, count), pl.ds(pad + g, SUB, stride=groups), slice(None))

    def note(k, target, tile, row):
        for cb in range(blocks):
            block = planes[target, tile, pl.ds(own + cb * TILE, TILE), :].T
            trace[cb, pl.ds(k, 1), :] = block[row : row + 1]

    def fluid_step(k, cur, other):
        source[...] = jnp.dot(wave_g[...], picks[k], preferred_element_type=F32)
        count = tiles + 1
        now, old, coef = planes.at[cur], planes.at[other], planes.at[2]
        prev, here = now[row_of(count, -1)], now[row_of(count, 0)]
        for g in range(groups):
            after = now[row_of(count, g + 1)]
            side_up, side_down = pltpu.roll(here[side], 1, 1), pltpu.roll(here[side], TILE - 1, 1)
            tail, head = pltpu.roll(here[tiles - 1], 1, 1), pltpu.roll(here[0], TILE - 1, 1)
            up = jnp.concatenate(
                [jnp.where(is_first, side_up, tail)[None], here[: tiles - 1],
                 jnp.where(is_first, tail, side_up)[None]], 0)
            part = slice(g * SUB, (g + 1) * SUB)
            down = jnp.concatenate(
                [here[1:tiles],
                 (jnp.where(is_last, side_down, head) + source[part, :TILE])[None],
                 (jnp.where(is_last, head, side_down) + source[part, TILE:])[None]], 0)
            near = (prev + after) + (up + down)
            at = row_of(count, g)
            old[at] = (scale[at] * here - old[at]) + coef[at] * near
            prev, here = here, after
        note(k, other, tiles - 1, TILE - 1)

    def shell_step(k, cur, other):
        inner = pl.ds(pad, wide)
        rounded = jnp.concatenate(
            [planes[cur, t, inner, :].astype(BF16) for t in range(tiles)], 1
        )
        result = jnp.dot(rounded, element[...], preferred_element_type=F32)
        for t in range(tiles):
            term[t, inner, :] = result[:, t * TILE : (t + 1) * TILE]
        source[:, :TILE] = jnp.dot(
            wave_g[...], picks[k, :, :TILE], preferred_element_type=F32
        )
        count = tiles
        now, old, coef = planes.at[cur], planes.at[other], planes.at[2]
        prev, here = now[row_of(count, -1)], now[row_of(count, 0)]
        for g in range(groups):
            after = now[row_of(count, g + 1)]
            tail, head = pltpu.roll(here[tiles - 1], 1, 1), pltpu.roll(here[0], TILE - 1, 1)
            part = slice(g * SUB, (g + 1) * SUB)
            up = jnp.concatenate(
                [(jnp.where(is_first, 0.0, tail) + source[part, :TILE])[None],
                 here[: tiles - 1]], 0)
            down = jnp.concatenate([here[1:tiles], jnp.where(is_last, 0.0, head)[None]], 0)
            at = row_of(count, g)
            near = (prev + after) + (up + down) - term[at]
            old[at] = (scale[at] * here - old[at]) + coef[at] * near
            prev, here = here, after
        note(k, other, 0, 0)

    def pair_of(step):
        def body(i, carry):
            step(2 * i, 0, 1)
            step(2 * i + 1, 1, 0)
            return carry

        lax.fori_loop(0, substeps // 2, body, 0)

    for ref in (planes.at[0], planes.at[1]):
        for t in range(tiles + 1):
            ref[t, pl.ds(0, pad), :] = jnp.zeros((pad, TILE), F32)
            ref[t, pl.ds(pad + wide, pad), :] = jnp.zeros((pad, TILE), F32)

    def hand_out():
        leave = []
        for a, target in ((0, state_out), (1, previous_out)):
            for cb in range(blocks):
                for t in range(tiles):
                    block = planes[a, t, pl.ds(own + cb * TILE, TILE), :].T
                    for m in range(TILE // SUB):
                        nat[a, cb, pl.ds(t + 4 * SUB * m, SUB, stride=tiles), :] = block[
                            m * SUB : (m + 1) * SUB
                        ]
                copy = pltpu.make_async_copy(
                    nat.at[a, cb], target.at[:, pl.ds(cb * TILE, TILE)],
                    out_sem.at[a * blocks + cb],
                )
                copy.start()
                leave.append(copy)
        return leave

    @pl.when(on_shell)
    def _():
        pair_of(shell_step)
        sends = []
        for t in range(shell):
            copy = remote(trace, shell_trace, down_send.at[t], down_recv, t, d)
            copy.start()
            sends.append(copy)
        nodes_out[...] = jnp.zeros_like(nodes_out)
        leave = hand_out()
        for t in range(shell):
            remote(total, parts.at[t], part_send, part_recv.at[t], t, d).wait_recv()
        sums = parts[0]
        for t in range(1, shell):
            sums = sums + parts[t]
        loads_out[...] = sums
        for copy in sends:
            copy.wait_send()
        for copy in leave:
            copy.wait()

    @pl.when(on_fluid)
    def _():
        pair_of(fluid_step)
        terms = []
        for e in range(entries):
            x_high, x_low = split(trace[face[e]])
            first = jnp.dot(
                jnp.concatenate([x_high, x_low], 0), w_high[e], preferred_element_type=F32
            )
            second = jnp.dot(x_high, w_low[e], preferred_element_type=F32)
            terms.append(first[:SUB] + first[SUB:] + second)
        high, low = split(jnp.concatenate(terms, 0))
        halves = jnp.concatenate([high, low], 1)
        size = blocks * SUB
        for o in range(0, n_dom * size, TILE):
            result = jnp.dot(onehot[pl.ds(o, TILE), :], halves, preferred_element_type=F32)
            result = result[:, :TILE] + result[:, TILE:]
            for j in range(TILE // size):
                for b in range(blocks):
                    at = j * size + b * SUB
                    outgoing[o // size + j, b] = result[at : at + SUB]
        sends = []
        for j in range(1, n_dom):
            to = lax.rem(d + j, n_dom)
            copy = remote(
                outgoing.at[to], arrived.at[j - 1], load_send.at[j - 1], load_recv.at[j - 1],
                s, to,
            )
            copy.start()
            sends.append(copy)
        remote(trace, shell_trace, down_send.at[0], down_recv, shell, d).wait_recv()
        spread = []
        for j in range(1, n_dom):
            to = lax.rem(d + j, n_dom)
            copy = remote(
                shell_trace, nodes.at[j - 1], node_send.at[j - 1], node_recv.at[j - 1], s, to
            )
            copy.start()
            spread.append(copy)
        leave = hand_out()
        value = outgoing[d]
        for j in range(1, n_dom):
            sends[j - 1].wait_recv()
            value = value + arrived[j - 1]
        total[...] = value
        up = remote(total, parts.at[s], part_send, part_recv.at[s], shell, d)
        up.start()
        loads_out[...] = jnp.zeros_like(loads_out)
        nodes_out[0] = shell_trace[...]
        for j in range(1, n_dom):
            spread[j - 1].wait_recv()
            nodes_out[j] = nodes[j - 1]
        for copy in sends + spread + [up]:
            copy.wait_send()
        for copy in leave:
            copy.wait()


def window(
    face, owner, node, state, previous, coefficient, stiffness, wave, rbf, n_sect, n_dom
):
    rows, lanes = state.shape
    substeps = wave.shape[0]
    entries, size = rbf.shape[0], rbf.shape[1]
    tiles, blocks = rows // TILE, lanes // TILE
    wide = lanes + 2 * HALO
    deep = wide + 2 * SUB
    smem = pl.BlockSpec(memory_space=pltpu.SMEM)
    anywhere = pl.BlockSpec(memory_space=pltpu.HBM)
    vmem = pl.BlockSpec(memory_space=pltpu.VMEM)
    dma = pltpu.SemaphoreType.DMA
    block = (blocks, substeps, size)

    def full(*shape, dtype=F32):
        return pltpu.VMEM(shape, dtype)

    return pl.pallas_call(
        functools.partial(window_kernel, n_sect, n_dom),
        out_shape=(
            jax.ShapeDtypeStruct((rows, lanes), F32),
            jax.ShapeDtypeStruct((rows, lanes), F32),
            jax.ShapeDtypeStruct(block, F32),
            jax.ShapeDtypeStruct((n_dom,) + block, F32),
        ),
        in_specs=[smem] * 3 + [anywhere] * 4 + [vmem] + [anywhere],
        out_specs=(anywhere, anywhere, vmem, vmem),
        scratch_shapes=[
            full(4, blocks, rows, TILE),
            full(3, tiles + 1, deep, TILE),
            full(tiles + 1, deep, TILE),
            full(deep, TILE),
            full(wide, TILE, dtype=BF16),
            full(substeps, TILE, 2 * TILE, dtype=BF16),
            full(wide, 2 * TILE),
            full(4, blocks + 2, HALO, TILE),
            full(3, blocks + 2, HALO, TILE),
            full(blocks + 2, HALO, TILE),
            full(*rbf.shape),
            full(*rbf.shape, dtype=BF16),
            full(*rbf.shape, dtype=BF16),
            full(n_dom * blocks * SUB, entries * SUB, dtype=BF16),
            full(*block),
            full(n_dom, *block),
            full(*stiffness.shape, dtype=BF16),
            full(rows, rows, dtype=BF16),
            full(tiles, TILE, TILE),
            full(tiles, deep, TILE),
            full(n_dom - 1, *block),
            full(*block),
            full(n_sect - 1, *block),
            full(n_dom - 1, *block),
            full(*block),
            dma((3 * blocks + 2,)),
            dma((2 * blocks,)),
            dma((10,)),
            dma((10,)),
            dma((n_dom - 1,)),
            dma((n_dom - 1,)),
            dma,
            dma((n_sect - 1,)),
            dma((n_sect - 1,)),
            dma,
            dma((n_dom - 1,)),
            dma((n_dom - 1,)),
        ],
        compiler_params=pltpu.CompilerParams(
            collective_id=0, has_side_effects=True, vmem_limit_bytes=60 * 1024 * 1024
        ),
        name="window",
    )(face, owner, node, state, previous, coefficient, stiffness, wave, rbf)


def three_products(x, high, low):
    x_high, x_low = split(x)
    dims = (((1,), (1,)), ((), ()))
    both = jnp.concatenate([x_high, x_low], 0)
    first = lax.dot_general(both, high, dims, preferred_element_type=F32)
    second = lax.dot_general(x_high, low, dims, preferred_element_type=F32)
    return first[:SUB] + first[SUB:] + second


def pull_kernel(
    n_sect, n_dom, face, owner, node, state, previous, loads, nodes, rbf,
    state_out, previous_out, out, weights, fields, terms, sums, sems,
):
    entries = rbf.shape[0]
    substeps = out.shape[0]
    blocks = loads.shape[0]
    d = lax.axis_index("dom")
    on_shell = lax.axis_index("sect") == n_sect - 1
    part = entries // PARTS
    maps = [
        pltpu.make_async_copy(
            rbf.at[pl.ds(i * part, part)], weights.at[pl.ds(i * part, part)], sems.at[i]
        )
        for i in range(PARTS)
    ]
    rows = state.shape[0] // PARTS
    enter, leave = [], []
    for a, (source, target) in enumerate(((state, state_out), (previous, previous_out))):
        for i in range(PARTS):
            piece = pl.ds(i * rows, rows)
            sem = sems.at[PARTS * (a + 1) + i]
            enter.append(pltpu.make_async_copy(source.at[piece], fields.at[a, piece], sem))
            leave.append(pltpu.make_async_copy(fields.at[a, piece], target.at[piece], sem))

    @pl.when(jnp.logical_not(on_shell))
    def _():
        for copy in maps:
            copy.start()

    for copy in enter:
        copy.start()

    def pass_on():
        for copy_in, copy_out in zip(enter, leave):
            copy_in.wait()
            copy_out.start()

    @pl.when(on_shell)
    def _():
        for b in range(blocks):
            for k in range(substeps):
                out[k, :, b * TILE : (b + 1) * TILE] = loads[b, k : k + 1, :]
        pass_on()

    @pl.when(jnp.logical_not(on_shell))
    def _():
        sums[...] = jnp.zeros_like(sums)
        for copy in maps:
            copy.wait()
        pass_on()
        for e in range(entries):
            slot = lax.rem(d - owner[e] + n_dom, n_dom)
            high, low = split(weights[e])
            terms[e] = three_products(nodes[slot, node[e]], high, low)
        for e in range(entries):
            sums[face[e]] += terms[e]
        for b in range(blocks):
            for k in range(substeps):
                out[k, :, b * TILE : (b + 1) * TILE] = sums[b, k : k + 1, :]

    for copy in leave:
        copy.wait()


def pull(face, owner, node, state, previous, loads, nodes, rbf, n_sect, n_dom):
    blocks, substeps, size = loads.shape
    smem = pl.BlockSpec(memory_space=pltpu.SMEM)
    anywhere = pl.BlockSpec(memory_space=pltpu.HBM)
    vmem = pl.BlockSpec(memory_space=pltpu.VMEM)
    return pl.pallas_call(
        functools.partial(pull_kernel, n_sect, n_dom),
        out_shape=(
            jax.ShapeDtypeStruct(state.shape, F32),
            jax.ShapeDtypeStruct(state.shape, F32),
            jax.ShapeDtypeStruct((substeps, 1, blocks * size), F32),
        ),
        in_specs=[smem] * 3 + [anywhere] * 2 + [vmem] * 2 + [anywhere],
        out_specs=(anywhere, anywhere, vmem),
        scratch_shapes=[
            pltpu.VMEM(rbf.shape, F32),
            pltpu.VMEM((2,) + state.shape, F32),
            pltpu.VMEM((rbf.shape[0], substeps, size), F32),
            pltpu.VMEM((blocks, substeps, size), F32),
            pltpu.SemaphoreType.DMA((3 * PARTS,)),
        ],
        compiler_params=pltpu.CompilerParams(vmem_limit_bytes=60 * 1024 * 1024),
        name="pull",
    )(face, owner, node, state, previous, loads, nodes, rbf)


def local(
    state, previous, coefficient, stiffness, waveform, entry_face, entry_owner, entry_node, rbf
):
    n_sect = lax.axis_size("sect")
    n_dom = lax.axis_size("dom")
    owner = entry_owner.reshape(entry_owner.shape[0])
    current, before, loads, nodes = window(
        entry_face, owner, entry_node, state, previous, coefficient, stiffness, waveform, rbf,
        n_sect, n_dom,
    )
    return pull(
        entry_face, owner, entry_node, current, before, loads, nodes, rbf, n_sect, n_dom
    )


def solution(mesh):
    in_specs = (
        P("sect", "dom"),
        P("sect", "dom"),
        P("sect", "dom"),
        P(),
        P(None, ("sect", "dom"), None),
        P(("sect", "dom")),
        P(("sect", "dom"), None),
        P(("sect", "dom")),
        P(("sect", "dom"), None, None),
    )
    out_specs = (P("sect", "dom"), P("sect", "dom"), P(None, ("sect", "dom"), None))
    return jax.shard_map(local, mesh=mesh, in_specs=in_specs, out_specs=out_specs, check_vma=False)
```

```python
import functools

import jax
import jax.numpy as jnp
from jax import lax
from jax.experimental import pallas as pl
from jax.experimental.pallas import tpu as pltpu
from jax.sharding import PartitionSpec as P

HALO = 8
TILE = 128
SUB = 8
F32 = jnp.float32
BF16 = jnp.bfloat16
MESH = pl.DeviceIdType.MESH


def remote(source, target, send, recv, section, column):
    return pltpu.make_async_remote_copy(
        src_ref=source,
        dst_ref=target,
        send_sem=send,
        recv_sem=recv,
        device_id=(section, column),
        device_id_type=MESH,
    )


def split(value):
    high = value.astype(BF16)
    low = (value - high.astype(F32)).astype(BF16)
    return high, low


def iota(shape, axis):
    return lax.broadcasted_iota(jnp.int32, shape, axis)


def window_kernel(
    n_sect, n_dom,
    face, owner, node, state, previous, coefficient, stiffness, wave_hbm, rbf,
    fields_out, loads_out, nodes_out, w_high, w_low,
    nat, planes, scale, wave_t, wave_g, picks, source, above, below, own_wave,
    weights, wave_ref, onehot, trace, outgoing, matrices, element, products,
    arrived, total, parts, nodes, shell_trace,
    load_sem, send_sem, recv_sem,
    load_send, load_recv, part_send, part_recv, down_send, down_recv, node_send, node_recv,
):
    rows, lanes = state.shape
    substeps = wave_hbm.shape[0]
    entries = rbf.shape[0]
    tiles = rows // TILE
    blocks = lanes // TILE
    wide = lanes + 2 * HALO
    groups = wide // SUB
    pad = SUB
    own = pad + HALO
    side = tiles
    s = lax.axis_index("sect")
    d = lax.axis_index("dom")
    shell = n_sect - 1
    on_shell = s == shell
    on_fluid = jnp.logical_not(on_shell)
    both = jnp.logical_and
    has_left = d > 0
    has_right = d < n_dom - 1
    has_up = both(s >= 1, s <= n_sect - 2)
    has_down = s <= n_sect - 3
    barrier = pltpu.get_barrier_semaphore()

    def greet(section, column):
        pl.semaphore_signal(barrier, inc=1, device_id=(section, column), device_id_type=MESH)

    diagonals = (
        (both(has_up, has_left), s - 1, d - 1),
        (both(has_up, has_right), s - 1, d + 1),
        (both(has_down, has_left), s + 1, d - 1),
        (both(has_down, has_right), s + 1, d + 1),
    )
    for has, section, column in ((has_up, s - 1, d), (has_down, s + 1, d)) + diagonals:

        @pl.when(has)
        def _(section=section, column=column):
            greet(section, column)

    @pl.when(on_fluid)
    def _():
        for j in range(1, n_dom):
            greet(s, lax.rem(d + j, n_dom))
        greet(shell, d)

    @pl.when(on_shell)
    def _():
        for t in range(shell):
            greet(t, d)

        @pl.when(has_left)
        def _():
            greet(s, d - 1)

        @pl.when(has_right)
        def _():
            greet(s, d + 1)

    def one(flag):
        return jnp.where(flag, 1, 0).astype(jnp.int32)

    sideways = one(has_left) + one(has_right)
    peers = one(has_up) + one(has_down) + sum(one(route[0]) for route in diagonals)
    peers = peers + jnp.where(on_shell, shell + sideways, n_dom).astype(jnp.int32)

    fields = (state, previous, coefficient)
    order = [0, blocks - 1] + list(range(1, blocks - 1))
    loads = {}
    for cb in order:
        for a in range(3):
            copy = pltpu.make_async_copy(
                fields[a].at[:, pl.ds(cb * TILE, TILE)], nat.at[a, cb],
                load_sem.at[a * blocks + cb],
            )
            copy.start()
            loads[a, cb] = copy
    elements = pltpu.make_async_copy(stiffness, matrices, load_sem.at[3 * blocks])
    elements.start()
    waves = pltpu.make_async_copy(wave_hbm, wave_ref, load_sem.at[3 * blocks + 2])
    waves.start()
    maps = pltpu.make_async_copy(rbf, weights, load_sem.at[3 * blocks + 1])
    maps.start()

    last_rows = pl.ds(rows - HALO, HALO)
    waves.wait()
    for cb in range(blocks):
        piece = jnp.concatenate(
            [wave_ref[k, :, cb * TILE : (cb + 1) * TILE] for k in range(substeps)], 0
        )
        nat[3, cb, last_rows, :] = piece
        own_wave[1 + cb] = piece

    half = tiles // 2

    def spot(t, m, spacing):
        start = t if spacing == tiles else t % half + t // half * (rows // 2)
        return pl.ds(start + spacing * SUB * m, SUB, stride=spacing)

    def lay_in(blocks_in, spacing):
        for cb in blocks_in:
            for a in range(3):
                for t in range(tiles):
                    block = jnp.concatenate(
                        [nat[a, cb, spot(t, m, spacing), :] for m in range(TILE // SUB)], 0
                    )
                    planes[a, t, pl.ds(own + cb * TILE, TILE), :] = block.T

    def turn(blocks_in):
        @pl.when(on_fluid)
        def _():
            lay_in(blocks_in, tiles)

        @pl.when(on_shell)
        def _():
            lay_in(blocks_in, half)

    for cb in order[:2]:
        for a in range(3):
            loads[a, cb].wait()
    turn(order[:2])

    def columns(start):
        return planes.at[:, pl.ds(0, tiles), pl.ds(start, HALO), :]

    first_rows = pl.ds(0, HALO)
    three = pl.ds(0, 3)
    middle = pl.ds(1, blocks)
    end = blocks - 1
    routes = (
        (has_left, s, d - 1, columns(own), columns(own + lanes),
         has_right, columns(own + lanes)),
        (has_right, s, d + 1, columns(own + lanes - HALO), columns(pad), has_left, columns(pad)),
        (has_up, s - 1, d, nat.at[three, :, first_rows, :], below.at[:, middle],
         has_down, below.at[:, middle]),
        (has_down, s + 1, d, nat.at[:, :, last_rows, :], above.at[:, middle],
         has_up, above.at[:, middle]),
        (diagonals[0][0], s - 1, d - 1, nat.at[three, 0, first_rows, :], below.at[:, blocks + 1],
         both(has_down, has_right), below.at[:, blocks + 1]),
        (diagonals[1][0], s - 1, d + 1, nat.at[three, end, first_rows, :], below.at[:, 0],
         both(has_down, has_left), below.at[:, 0]),
        (diagonals[2][0], s + 1, d - 1, nat.at[:, 0, last_rows, :], above.at[:, blocks + 1],
         both(has_up, has_right), above.at[:, blocks + 1]),
        (diagonals[3][0], s + 1, d + 1, nat.at[:, end, last_rows, :], above.at[:, 0],
         both(has_up, has_left), above.at[:, 0]),
        (has_left, s, d - 1, nat.at[3, 0, last_rows, :], own_wave.at[blocks + 1],
         has_right, own_wave.at[blocks + 1]),
        (has_right, s, d + 1, nat.at[3, end, last_rows, :], own_wave.at[0],
         has_left, own_wave.at[0]),
    )

    for cb in order[2:]:
        for a in range(3):
            loads[a, cb].wait()
    pl.semaphore_wait(barrier, peers)
    copies = []
    for i, (has, section, column, source_ref, target_ref, _, _) in enumerate(routes):
        copy = remote(source_ref, target_ref, send_sem.at[i], recv_sem.at[i], section, column)
        copies.append(copy)

        @pl.when(has)
        def _(copy=copy):
            copy.start()

    turn(order[2:])

    def prepare(t, start, count):
        part = pl.ds(start, count)
        scale[t, part, :] = 2.0 - 4.0 * planes[2, t, part, :]

    for t in range(tiles):
        prepare(t, own, lanes)

    at_own = jnp.where(on_shell, 0, TILE - 1).astype(jnp.int32)
    sign = jnp.where(on_shell, -1.0, 1.0).astype(F32)
    lane = iota((TILE, 2 * TILE), 0)
    goal = iota((TILE, 2 * TILE), 1)
    for k in range(substeps):
        mine = jnp.logical_or(lane == 40 + k, lane == 56 + k)
        upper = jnp.logical_or(lane == 48 + k, lane == 64 + k)
        hit = jnp.logical_or(both(mine, goal == at_own), both(upper, goal == 2 * TILE - 1))
        picks[k] = jnp.where(hit, sign, 0.0).astype(BF16)

    elements.wait()

    @pl.when(on_shell)
    def _():
        width = TILE // half
        for b in range(tiles):
            i = iota((TILE, rows // 2), 0)
            n = iota((TILE, rows // 2), 1)
            place = lax.rem(i, half) * TILE + width * (b % half) + i // half
            spread = jnp.where(n == place, 1.0, 0.0).astype(BF16)
            wide_rows = jnp.dot(matrices[b], spread, preferred_element_type=F32)
            for u in range(half):
                products[u] = wide_rows[:, u * TILE : (u + 1) * TILE]
            for t in range(half):
                for u in range(half):
                    start = t * TILE + width * (b % half)
                    element[b // half, pl.ds(start, width), pl.ds(u * TILE, TILE)] = products[
                        u, pl.ds(t, width, stride=half), :
                    ].astype(BF16)

    maps.wait()

    @pl.when(on_fluid)
    def _():
        lanes_e = iota((SUB, entries * SUB), 1)
        goal = jnp.zeros((SUB, entries * SUB), jnp.int32)
        for e in range(entries):
            slot = owner[e] * blocks + node[e]
            goal = jnp.where(lanes_e // SUB == e, slot, goal)
        goal = goal * SUB + lax.rem(lanes_e, SUB)
        size = n_dom * blocks * SUB
        for r in range(0, size, TILE):
            here = iota((TILE, entries * SUB), 0) + r
            onehot[pl.ds(r, TILE), :] = jnp.where(here == goal[0:1, :], 1.0, 0.0).astype(BF16)
        for e in range(entries):
            high, low = split(weights[e])
            w_high[e] = high
            w_low[e] = low

    for i, (_, _, _, _, _, comes, buf) in enumerate(routes):

        @pl.when(comes)
        def _(copy=copies[i]):
            copy.wait_recv()

        @pl.when(jnp.logical_not(comes))
        def _(buf=buf):
            buf[...] = jnp.zeros(buf.shape, F32)

    for t in range(tiles):
        prepare(t, pad, HALO)
        prepare(t, own + lanes, HALO)

    edge = iota((HALO, TILE), 1)
    empty = jnp.zeros((TILE - 8 * HALO, TILE), F32)

    def joined(ref):
        if ref[1] is not None:
            right, left = ref[0][ref[1], blocks + 1], ref[0][ref[1], 0]
        else:
            right, left = ref[0][blocks + 1], ref[0][0]
        return jnp.where(edge < HALO, right, jnp.where(edge >= TILE - HALO, left, 0.0))

    def straight(q):
        def pick(ref):
            return ref[0][ref[1], q] if ref[1] is not None else ref[0][q]

        return pick

    def stacked(pick):
        parts_list = [
            pick((below, 0)), pick((above, 1)), pick((below, 1)), pick((above, 2)),
            pick((below, 2)), pick((own_wave, None)), pick((above, 3)), empty, pick((above, 0)),
        ]
        return jnp.concatenate(parts_list, 0).T

    def lay(block, start, count, base):
        part = pl.ds(start, count)
        cut = block[base : base + count]
        planes[0, side, part, :] = cut
        planes[1, side, part, :] = pltpu.roll(cut, TILE - 2 * HALO, 1)
        coef = pltpu.roll(cut, TILE - 4 * HALO, 1)
        planes[2, side, part, :] = coef
        scale[side, part, :] = 2.0 - 4.0 * coef
        at = iota((count, TILE), 1)
        keep = both(at >= 5 * HALO, at < 7 * HALO)
        wave_t[part, :] = jnp.where(keep, cut, 0.0)

    for q in range(blocks):
        lay(stacked(straight(1 + q)), own + q * TILE, TILE, 0)
    corner = stacked(joined)
    lay(corner, own + lanes, HALO, 0)
    lay(corner, pad, HALO, TILE - HALO)

    for g in range(0, groups, 2):
        pair = jnp.concatenate(
            [wave_t[pl.ds(pad + g + i, SUB, stride=groups), :] for i in range(2)], 0
        )
        high = pair.astype(BF16).astype(F32)
        low = pltpu.roll(pair - high, 2 * HALO, 1)
        wave_g[pl.ds(g * SUB, 2 * SUB), :] = (high + low).astype(BF16)

    for i, route in enumerate(routes):

        @pl.when(route[0])
        def _(copy=copies[i]):
            copy.wait_send()

    lane8 = iota((SUB, TILE), 1)
    is_first = lane8 == 0
    is_last = lane8 == TILE - 1

    def row_of(count, g):
        return (pl.ds(0, count), pl.ds(pad + g, SUB, stride=groups), slice(None))

    def note(k, target, tile, row):
        for cb in range(blocks):
            block = planes[target, tile, pl.ds(own + cb * TILE, TILE), :].T
            trace[cb, pl.ds(k, 1), :] = block[row : row + 1]

    def fluid_step(k, cur, other):
        source[...] = jnp.dot(wave_g[...], picks[k], preferred_element_type=F32)
        count = tiles + 1
        now, old, coef = planes.at[cur], planes.at[other], planes.at[2]
        prev, here = now[row_of(count, -1)], now[row_of(count, 0)]
        for g in range(groups):
            after = now[row_of(count, g + 1)]
            side_up, side_down = pltpu.roll(here[side], 1, 1), pltpu.roll(here[side], TILE - 1, 1)
            tail, head = pltpu.roll(here[tiles - 1], 1, 1), pltpu.roll(here[0], TILE - 1, 1)
            up = jnp.concatenate(
                [jnp.where(is_first, side_up, tail)[None], here[: tiles - 1],
                 jnp.where(is_first, tail, side_up)[None]], 0)
            part = slice(g * SUB, (g + 1) * SUB)
            down = jnp.concatenate(
                [here[1:tiles],
                 (jnp.where(is_last, side_down, head) + source[part, :TILE])[None],
                 (jnp.where(is_last, head, side_down) + source[part, TILE:])[None]], 0)
            near = (prev + after) + (up + down)
            at = row_of(count, g)
            old[at] = (scale[at] * here - old[at]) + coef[at] * near
            prev, here = here, after
        note(k, other, tiles - 1, TILE - 1)

    def shell_step(k, cur, other):
        now, old, coef = planes.at[cur], planes.at[other], planes.at[2]
        terms = []
        for u in range(2):
            x = jnp.concatenate(
                [jnp.concatenate(
                    [now[u * half + t, pl.ds(pad + g, SUB, stride=groups), :]
                     for g in range(groups)], 0,
                ).astype(BF16) for t in range(half)], 1,
            )
            matrix = element[u]
            if u == 0:
                x = jnp.concatenate([x, wave_g[...]], 1)
                matrix = jnp.concatenate([matrix, picks[k]], 0)
            terms.append(jnp.dot(x, matrix, preferred_element_type=F32))

        def row(g):
            return [now[t, pl.ds(pad + g, SUB, stride=groups), :] for t in range(tiles)]

        prev, here = row(-1), row(0)
        for g in range(groups):
            after = row(g + 1)
            tails = [pltpu.roll(here[u * half + half - 1], 1, 1) for u in range(2)]
            heads = [pltpu.roll(here[u * half], TILE - 1, 1) for u in range(2)]
            for t in range(tiles):
                u, within = t // half, t % half
                if within:
                    up = here[t - 1]
                else:
                    up = jnp.where(is_first, tails[u - 1] if u else 0.0, tails[u])
                if within < half - 1:
                    down = here[t + 1]
                else:
                    down = jnp.where(is_last, 0.0 if u else heads[1], heads[u])
                term = terms[u][g * SUB : (g + 1) * SUB, within * TILE : (within + 1) * TILE]
                near = (prev[t] + after[t]) + (up + down) - term
                at = (t, pl.ds(pad + g, SUB, stride=groups), slice(None))
                old[at] = (scale[at] * here[t] - old[at]) + coef[at] * near
            prev, here = here, after
        note(k, other, 0, 0)

    def pair_of(step):
        def body(i, carry):
            step(2 * i, 0, 1)
            step(2 * i + 1, 1, 0)
            return carry

        lax.fori_loop(0, substeps // 2, body, 0)

    for ref in (planes.at[0], planes.at[1]):
        for t in range(tiles + 1):
            ref[t, pl.ds(0, pad), :] = jnp.zeros((pad, TILE), F32)
            ref[t, pl.ds(pad + wide, pad), :] = jnp.zeros((pad, TILE), F32)

    def hand_out(spacing):
        for a in range(2):
            for cb in range(blocks):
                for t in range(tiles):
                    block = planes[a, t, pl.ds(own + cb * TILE, TILE), :].T
                    for m in range(TILE // SUB):
                        fields_out[a, cb, spot(t, m, spacing), :] = block[
                            m * SUB : (m + 1) * SUB
                        ]

    @pl.when(on_shell)
    def _():
        pair_of(shell_step)
        sends = []
        for t in range(shell):
            copy = remote(trace, shell_trace, down_send.at[t], down_recv, t, d)
            copy.start()
            sends.append(copy)
        nodes_out[...] = jnp.zeros_like(nodes_out)
        hand_out(half)
        for t in range(shell):
            remote(total, parts.at[t], part_send, part_recv.at[t], t, d).wait_recv()
        sums = parts[0]
        for t in range(1, shell):
            sums = sums + parts[t]
        loads_out[...] = sums
        for copy in sends:
            copy.wait_send()

    @pl.when(on_fluid)
    def _():
        pair_of(fluid_step)
        terms = []
        for e in range(entries):
            x_high, x_low = split(trace[face[e]])
            first = jnp.dot(
                jnp.concatenate([x_high, x_low], 0), w_high[e], preferred_element_type=F32
            )
            second = jnp.dot(x_high, w_low[e], preferred_element_type=F32)
            terms.append(first[:SUB] + first[SUB:] + second)
        high, low = split(jnp.concatenate(terms, 0))
        halves = jnp.concatenate([high, low], 1)
        size = blocks * SUB
        for o in range(0, n_dom * size, TILE):
            result = jnp.dot(onehot[pl.ds(o, TILE), :], halves, preferred_element_type=F32)
            result = result[:, :TILE] + result[:, TILE:]
            for j in range(TILE // size):
                for b in range(blocks):
                    at = j * size + b * SUB
                    outgoing[o // size + j, b] = result[at : at + SUB]
        sends = []
        for j in range(1, n_dom):
            to = lax.rem(d + j, n_dom)
            copy = remote(
                outgoing.at[to], arrived.at[j - 1], load_send.at[j - 1], load_recv.at[j - 1],
                s, to,
            )
            copy.start()
            sends.append(copy)
        remote(trace, shell_trace, down_send.at[0], down_recv, shell, d).wait_recv()
        spread = []
        for j in range(1, n_dom):
            to = lax.rem(d + j, n_dom)
            copy = remote(
                shell_trace, nodes.at[j - 1], node_send.at[j - 1], node_recv.at[j - 1], s, to
            )
            copy.start()
            spread.append(copy)
        hand_out(tiles)
        value = outgoing[d]
        for j in range(1, n_dom):
            sends[j - 1].wait_recv()
            value = value + arrived[j - 1]
        total[...] = value
        up = remote(total, parts.at[s], part_send, part_recv.at[s], shell, d)
        up.start()
        loads_out[...] = jnp.zeros_like(loads_out)
        nodes_out[0] = shell_trace[...]
        for j in range(1, n_dom):
            spread[j - 1].wait_recv()
            nodes_out[j] = nodes[j - 1]
        for copy in sends + spread + [up]:
            copy.wait_send()


def window(
    face, owner, node, state, previous, coefficient, stiffness, wave, rbf, n_sect, n_dom
):
    rows, lanes = state.shape
    substeps = wave.shape[0]
    entries, size = rbf.shape[0], rbf.shape[1]
    tiles, blocks = rows // TILE, lanes // TILE
    wide = lanes + 2 * HALO
    deep = wide + 2 * SUB
    smem = pl.BlockSpec(memory_space=pltpu.SMEM)
    anywhere = pl.BlockSpec(memory_space=pltpu.HBM)
    vmem = pl.BlockSpec(memory_space=pltpu.VMEM)
    dma = pltpu.SemaphoreType.DMA
    block = (blocks, substeps, size)
    held = [
        pltpu.with_memory_space_constraint(x, pltpu.HBM)
        for x in (state, previous, coefficient, stiffness, wave, rbf)
    ]

    def full(*shape, dtype=F32):
        return pltpu.VMEM(shape, dtype)

    return pl.pallas_call(
        functools.partial(window_kernel, n_sect, n_dom),
        out_shape=(
            pltpu.VMEM((2, blocks, rows, TILE), F32),
            pltpu.VMEM(block, F32),
            pltpu.VMEM((n_dom,) + block, F32),
            pltpu.VMEM(rbf.shape, BF16),
            pltpu.VMEM(rbf.shape, BF16),
        ),
        in_specs=[smem] * 3 + [anywhere] * 6,
        out_specs=(vmem,) * 5,
        scratch_shapes=[
            full(4, blocks, rows, TILE),
            full(3, tiles + 1, deep, TILE),
            full(tiles + 1, deep, TILE),
            full(deep, TILE),
            full(wide, TILE, dtype=BF16),
            full(substeps, TILE, 2 * TILE, dtype=BF16),
            full(wide, 2 * TILE),
            full(4, blocks + 2, HALO, TILE),
            full(3, blocks + 2, HALO, TILE),
            full(blocks + 2, HALO, TILE),
            full(*rbf.shape),
            full(*wave.shape),
            full(n_dom * blocks * SUB, entries * SUB, dtype=BF16),
            full(*block),
            full(n_dom, *block),
            full(*stiffness.shape, dtype=BF16),
            full(2, rows // 2, rows // 2, dtype=BF16),
            full(tiles // 2, TILE, TILE),
            full(n_dom - 1, *block),
            full(*block),
            full(n_sect - 1, *block),
            full(n_dom - 1, *block),
            full(*block),
            dma((3 * blocks + 3,)),
            dma((10,)),
            dma((10,)),
            dma((n_dom - 1,)),
            dma((n_dom - 1,)),
            dma,
            dma((n_sect - 1,)),
            dma((n_sect - 1,)),
            dma,
            dma((n_dom - 1,)),
            dma((n_dom - 1,)),
        ],
        compiler_params=pltpu.CompilerParams(
            collective_id=0, has_side_effects=True, vmem_limit_bytes=59 * 1024 * 1024
        ),
        name="window",
    )(face, owner, node, *held)


def three_products(x, high, low):
    x_high, x_low = split(x)
    dims = (((1,), (1,)), ((), ()))
    both = jnp.concatenate([x_high, x_low], 0)
    first = lax.dot_general(both, high, dims, preferred_element_type=F32)
    second = lax.dot_general(x_high, low, dims, preferred_element_type=F32)
    return first[:SUB] + first[SUB:] + second


def pull_kernel(
    n_sect, n_dom, face, owner, node, fields, loads, nodes, w_high, w_low,
    state_out, previous_out, out, terms, sums, sems,
):
    entries = w_high.shape[0]
    substeps = out.shape[0]
    blocks = loads.shape[0]
    d = lax.axis_index("dom")
    on_shell = lax.axis_index("sect") == n_sect - 1
    leave = [
        pltpu.make_async_copy(
            fields.at[a, cb], target.at[:, pl.ds(cb * TILE, TILE)], sems.at[a * blocks + cb]
        )
        for a, target in enumerate((state_out, previous_out))
        for cb in range(blocks)
    ]
    for copy in leave:
        copy.start()

    @pl.when(on_shell)
    def _():
        for b in range(blocks):
            for k in range(substeps):
                out[k, :, b * TILE : (b + 1) * TILE] = loads[b, k : k + 1, :]

    @pl.when(jnp.logical_not(on_shell))
    def _():
        sums[...] = jnp.zeros_like(sums)
        for e in range(entries):
            slot = lax.rem(d - owner[e] + n_dom, n_dom)
            terms[e] = three_products(nodes[slot, node[e]], w_high[e], w_low[e])
        for e in range(entries):
            sums[face[e]] += terms[e]
        for b in range(blocks):
            for k in range(substeps):
                out[k, :, b * TILE : (b + 1) * TILE] = sums[b, k : k + 1, :]

    for copy in leave:
        copy.wait()


def pull(face, owner, node, fields, loads, nodes, w_high, w_low, n_sect, n_dom):
    _, blocks, rows, size = fields.shape
    substeps = loads.shape[1]
    lanes = blocks * size
    smem = pl.BlockSpec(memory_space=pltpu.SMEM)
    hbm = pl.BlockSpec(memory_space=pltpu.HBM)
    vmem = pl.BlockSpec(memory_space=pltpu.VMEM)
    held = [
        pltpu.with_memory_space_constraint(x, pltpu.VMEM)
        for x in (fields, loads, nodes, w_high, w_low)
    ]
    return pl.pallas_call(
        functools.partial(pull_kernel, n_sect, n_dom),
        out_shape=(
            jax.ShapeDtypeStruct((rows, lanes), F32),
            jax.ShapeDtypeStruct((rows, lanes), F32),
            jax.ShapeDtypeStruct((substeps, 1, lanes), F32),
        ),
        in_specs=[smem] * 3 + [vmem] * 5,
        out_specs=(hbm, hbm, vmem),
        scratch_shapes=[
            pltpu.VMEM((w_high.shape[0], substeps, size), F32),
            pltpu.VMEM((blocks, substeps, size), F32),
            pltpu.SemaphoreType.DMA((2 * blocks,)),
        ],
        compiler_params=pltpu.CompilerParams(vmem_limit_bytes=16 * 1024 * 1024),
        name="pull",
    )(face, owner, node, *held)


def local(
    state, previous, coefficient, stiffness, waveform, entry_face, entry_owner, entry_node, rbf
):
    n_sect = lax.axis_size("sect")
    n_dom = lax.axis_size("dom")
    owner = entry_owner.reshape(entry_owner.shape[0])
    fields, loads, nodes, w_high, w_low = window(
        entry_face, owner, entry_node, state, previous, coefficient, stiffness, waveform, rbf,
        n_sect, n_dom,
    )
    return pull(
        entry_face, owner, entry_node, fields, loads, nodes, w_high, w_low, n_sect, n_dom
    )


def solution(mesh):
    in_specs = (
        P("sect", "dom"),
        P("sect", "dom"),
        P("sect", "dom"),
        P(),
        P(None, ("sect", "dom"), None),
        P(("sect", "dom")),
        P(("sect", "dom"), None),
        P(("sect", "dom")),
        P(("sect", "dom"), None, None),
    )
    out_specs = (P("sect", "dom"), P("sect", "dom"), P(None, ("sect", "dom"), None))
    return jax.shard_map(local, mesh=mesh, in_specs=in_specs, out_specs=out_specs, check_vma=False)
```

```python
import functools

import jax
import jax.numpy as jnp
from jax import lax
from jax.experimental import pallas as pl
from jax.experimental.pallas import tpu as pltpu
from jax.sharding import PartitionSpec as P

HALO = 8
TILE = 128
SUB = 8
F32 = jnp.float32
BF16 = jnp.bfloat16
MESH = pl.DeviceIdType.MESH
PIECES = 2


def remote(source, target, send, recv, section, column):
    return pltpu.make_async_remote_copy(
        src_ref=source,
        dst_ref=target,
        send_sem=send,
        recv_sem=recv,
        device_id=(section, column),
        device_id_type=MESH,
    )


def split(value):
    high = value.astype(BF16)
    low = (value - high.astype(F32)).astype(BF16)
    return high, low


def iota(shape, axis):
    return lax.broadcasted_iota(jnp.int32, shape, axis)


def window_kernel(
    n_sect, n_dom,
    face, owner, node, state, previous, coefficient, stiffness, wave_hbm, rbf,
    fields_out, loads_out, nodes_out, w_high, w_low,
    nat, planes, scale, wave_t, wave_g, picks, source, above, below, own_wave,
    weights, wave_ref, onehot, trace, outgoing, matrices, element, products,
    arrived, total, parts, nodes, pieces, shell_pieces,
    load_sem, send_sem, recv_sem,
    load_send, load_recv, part_send, part_recv, down_send, down_recv, node_send, node_recv,
    ready,
):
    rows, lanes = state.shape
    substeps = wave_hbm.shape[0]
    entries = rbf.shape[0]
    tiles = rows // TILE
    blocks = lanes // TILE
    wide = lanes + 2 * HALO
    groups = wide // SUB
    pad = SUB
    own = pad + HALO
    side = tiles
    s = lax.axis_index("sect")
    d = lax.axis_index("dom")
    shell = n_sect - 1
    on_shell = s == shell
    on_fluid = jnp.logical_not(on_shell)
    both = jnp.logical_and
    has_left = d > 0
    has_right = d < n_dom - 1
    has_up = both(s >= 1, s <= n_sect - 2)
    has_down = s <= n_sect - 3
    barrier = pltpu.get_barrier_semaphore()

    def greet(section, column):
        pl.semaphore_signal(barrier, inc=1, device_id=(section, column), device_id_type=MESH)

    diagonals = (
        (both(has_up, has_left), s - 1, d - 1),
        (both(has_up, has_right), s - 1, d + 1),
        (both(has_down, has_left), s + 1, d - 1),
        (both(has_down, has_right), s + 1, d + 1),
    )
    for has, section, column in ((has_up, s - 1, d), (has_down, s + 1, d)) + diagonals:

        @pl.when(has)
        def _(section=section, column=column):
            greet(section, column)

    @pl.when(on_fluid)
    def _():
        for j in range(1, n_dom):
            greet(s, lax.rem(d + j, n_dom))
        greet(shell, d)

    @pl.when(on_shell)
    def _():
        @pl.when(has_left)
        def _():
            greet(s, d - 1)

        @pl.when(has_right)
        def _():
            greet(s, d + 1)

    def one(flag):
        return jnp.where(flag, 1, 0).astype(jnp.int32)

    sideways = one(has_left) + one(has_right)
    peers = one(has_up) + one(has_down) + sum(one(route[0]) for route in diagonals)
    peers = peers + jnp.where(on_shell, shell + sideways, n_dom - 1).astype(jnp.int32)

    fields = (state, previous, coefficient)
    order = [0, blocks - 1] + list(range(1, blocks - 1))
    waves = pltpu.make_async_copy(wave_hbm, wave_ref, load_sem.at[3 * blocks + 2])
    waves.start()
    loads = {}
    for cb in order:
        for a in range(3):
            copy = pltpu.make_async_copy(
                fields[a].at[:, pl.ds(cb * TILE, TILE)], nat.at[a, cb],
                load_sem.at[a * blocks + cb],
            )
            copy.start()
            loads[a, cb] = copy
    elements = pltpu.make_async_copy(stiffness, matrices, load_sem.at[3 * blocks])
    elements.start()
    maps = pltpu.make_async_copy(rbf, weights, load_sem.at[3 * blocks + 1])

    last_rows = pl.ds(rows - HALO, HALO)
    waves.wait()
    for cb in range(blocks):
        piece = jnp.concatenate(
            [wave_ref[k, :, cb * TILE : (cb + 1) * TILE] for k in range(substeps)], 0
        )
        nat[3, cb, last_rows, :] = piece
        own_wave[1 + cb] = piece

    half = tiles // 2
    deep = substeps // PIECES

    def spot(t, m, spacing):
        start = t if spacing == tiles else t % half + t // half * (rows // 2)
        return pl.ds(start + spacing * SUB * m, SUB, stride=spacing)

    def lay_in(blocks_in, spacing):
        for cb in blocks_in:
            for a in range(3):
                for t in range(tiles):
                    block = jnp.concatenate(
                        [nat[a, cb, spot(t, m, spacing), :] for m in range(TILE // SUB)], 0
                    )
                    planes[a, t, pl.ds(own + cb * TILE, TILE), :] = block.T

    def turn(blocks_in):
        @pl.when(on_fluid)
        def _():
            lay_in(blocks_in, tiles)

        @pl.when(on_shell)
        def _():
            lay_in(blocks_in, half)

    for cb in order[:2]:
        for a in range(3):
            loads[a, cb].wait()
    turn(order[:2])

    def columns(start):
        return planes.at[:, pl.ds(0, tiles), pl.ds(start, HALO), :]

    first_rows = pl.ds(0, HALO)
    three = pl.ds(0, 3)
    middle = pl.ds(1, blocks)
    end = blocks - 1
    routes = (
        (has_left, s, d - 1, columns(own), columns(own + lanes),
         has_right, columns(own + lanes)),
        (has_right, s, d + 1, columns(own + lanes - HALO), columns(pad), has_left, columns(pad)),
        (has_left, s, d - 1, nat.at[3, 0, last_rows, :], own_wave.at[blocks + 1],
         has_right, own_wave.at[blocks + 1]),
        (has_right, s, d + 1, nat.at[3, end, last_rows, :], own_wave.at[0],
         has_left, own_wave.at[0]),
        (has_up, s - 1, d, nat.at[three, :, first_rows, :], below.at[:, middle],
         has_down, below.at[:, middle]),
        (has_down, s + 1, d, nat.at[:, :, last_rows, :], above.at[:, middle],
         has_up, above.at[:, middle]),
        (diagonals[0][0], s - 1, d - 1, nat.at[three, 0, first_rows, :], below.at[:, blocks + 1],
         both(has_down, has_right), below.at[:, blocks + 1]),
        (diagonals[1][0], s - 1, d + 1, nat.at[three, end, first_rows, :], below.at[:, 0],
         both(has_down, has_left), below.at[:, 0]),
        (diagonals[2][0], s + 1, d - 1, nat.at[:, 0, last_rows, :], above.at[:, blocks + 1],
         both(has_up, has_right), above.at[:, blocks + 1]),
        (diagonals[3][0], s + 1, d + 1, nat.at[:, end, last_rows, :], above.at[:, 0],
         both(has_up, has_left), above.at[:, 0]),
    )

    pl.semaphore_wait(barrier, peers)

    @pl.when(on_shell)
    def _():
        for t in range(shell):
            pl.semaphore_signal(ready, inc=1, device_id=(t, d), device_id_type=MESH)

    copies = []
    for i, (has, section, column, source_ref, target_ref, _, _) in enumerate(routes):
        if i == 4:
            for cb in order[2:]:
                for a in range(3):
                    loads[a, cb].wait()
        copy = remote(source_ref, target_ref, send_sem.at[i], recv_sem.at[i], section, column)
        copies.append(copy)

        @pl.when(has)
        def _(copy=copy):
            copy.start()

    @pl.when(on_fluid)
    def _():
        maps.start()

    turn(order[2:])

    def prepare(t, start, count):
        part = pl.ds(start, count)
        scale[t, part, :] = 2.0 - 4.0 * planes[2, t, part, :]

    for t in range(tiles):
        prepare(t, own, lanes)

    at_own = jnp.where(on_shell, 0, TILE - 1).astype(jnp.int32)
    sign = jnp.where(on_shell, -1.0, 1.0).astype(F32)
    lane = iota((TILE, 2 * TILE), 0)
    goal = iota((TILE, 2 * TILE), 1)
    for k in range(substeps):
        mine = jnp.logical_or(lane == 40 + k, lane == 56 + k)
        upper = jnp.logical_or(lane == 48 + k, lane == 64 + k)
        hit = jnp.logical_or(both(mine, goal == at_own), both(upper, goal == 2 * TILE - 1))
        picks[k] = jnp.where(hit, sign, 0.0).astype(BF16)

    elements.wait()

    @pl.when(on_shell)
    def _():
        width = TILE // half
        for b in range(tiles):
            i = iota((TILE, rows // 2), 0)
            n = iota((TILE, rows // 2), 1)
            place = lax.rem(i, half) * TILE + width * (b % half) + i // half
            spread = jnp.where(n == place, 1.0, 0.0).astype(BF16)
            wide_rows = jnp.dot(matrices[b], spread, preferred_element_type=F32)
            for u in range(half):
                products[u] = wide_rows[:, u * TILE : (u + 1) * TILE]
            for t in range(half):
                for u in range(half):
                    start = t * TILE + width * (b % half)
                    element[b // half, pl.ds(start, width), pl.ds(u * TILE, TILE)] = products[
                        u, pl.ds(t, width, stride=half), :
                    ].astype(BF16)

    @pl.when(on_fluid)
    def _():
        lanes_e = iota((SUB, entries * SUB), 1)
        goal = jnp.zeros((SUB, entries * SUB), jnp.int32)
        for e in range(entries):
            slot = owner[e] * blocks + node[e]
            goal = jnp.where(lanes_e // SUB == e, slot, goal)
        goal = goal * SUB + lax.rem(lanes_e, SUB)
        size = n_dom * blocks * SUB
        for r in range(0, size, TILE):
            here = iota((TILE, entries * SUB), 0) + r
            onehot[pl.ds(r, TILE), :] = jnp.where(here == goal[0:1, :], 1.0, 0.0).astype(BF16)
        maps.wait()
        for e in range(entries):
            high, low = split(weights[e])
            w_high[e] = high
            w_low[e] = low

    for i, (_, _, _, _, _, comes, buf) in enumerate(routes):

        @pl.when(comes)
        def _(copy=copies[i]):
            copy.wait_recv()

        @pl.when(jnp.logical_not(comes))
        def _(buf=buf):
            buf[...] = jnp.zeros(buf.shape, F32)

    for t in range(tiles):
        prepare(t, pad, HALO)
        prepare(t, own + lanes, HALO)

    edge = iota((HALO, TILE), 1)
    empty = jnp.zeros((TILE - 8 * HALO, TILE), F32)

    def joined(ref):
        if ref[1] is not None:
            right, left = ref[0][ref[1], blocks + 1], ref[0][ref[1], 0]
        else:
            right, left = ref[0][blocks + 1], ref[0][0]
        return jnp.where(edge < HALO, right, jnp.where(edge >= TILE - HALO, left, 0.0))

    def straight(q):
        def pick(ref):
            return ref[0][ref[1], q] if ref[1] is not None else ref[0][q]

        return pick

    def stacked(pick):
        parts_list = [
            pick((below, 0)), pick((above, 1)), pick((below, 1)), pick((above, 2)),
            pick((below, 2)), pick((own_wave, None)), pick((above, 3)), empty, pick((above, 0)),
        ]
        return jnp.concatenate(parts_list, 0).T

    def lay(block, start, count, base):
        part = pl.ds(start, count)
        cut = block[base : base + count]
        planes[0, side, part, :] = cut
        planes[1, side, part, :] = pltpu.roll(cut, TILE - 2 * HALO, 1)
        coef = pltpu.roll(cut, TILE - 4 * HALO, 1)
        planes[2, side, part, :] = coef
        scale[side, part, :] = 2.0 - 4.0 * coef
        at = iota((count, TILE), 1)
        keep = both(at >= 5 * HALO, at < 7 * HALO)
        wave_t[part, :] = jnp.where(keep, cut, 0.0)

    for q in range(blocks):
        lay(stacked(straight(1 + q)), own + q * TILE, TILE, 0)
    corner = stacked(joined)
    lay(corner, own + lanes, HALO, 0)
    lay(corner, pad, HALO, TILE - HALO)

    for g in range(0, groups, 2):
        pair = jnp.concatenate(
            [wave_t[pl.ds(pad + g + i, SUB, stride=groups), :] for i in range(2)], 0
        )
        high = pair.astype(BF16).astype(F32)
        low = pltpu.roll(pair - high, 2 * HALO, 1)
        wave_g[pl.ds(g * SUB, 2 * SUB), :] = (high + low).astype(BF16)

    for i, route in enumerate(routes):

        @pl.when(route[0])
        def _(copy=copies[i]):
            copy.wait_send()

    lane8 = iota((SUB, TILE), 1)
    is_first = lane8 == 0
    is_last = lane8 == TILE - 1

    def row_of(count, g):
        return (pl.ds(0, count), pl.ds(pad + g, SUB, stride=groups), slice(None))

    def interface(target, tile, row):
        for cb in range(blocks):
            yield cb, planes[target, tile, pl.ds(own + cb * TILE, TILE), :].T[row : row + 1]

    def fluid_step(k, cur, other):
        source[...] = jnp.dot(wave_g[...], picks[k], preferred_element_type=F32)
        count = tiles + 1
        now, old, coef = planes.at[cur], planes.at[other], planes.at[2]
        prev, here = now[row_of(count, -1)], now[row_of(count, 0)]
        for g in range(groups):
            after = now[row_of(count, g + 1)]
            side_up, side_down = pltpu.roll(here[side], 1, 1), pltpu.roll(here[side], TILE - 1, 1)
            tail, head = pltpu.roll(here[tiles - 1], 1, 1), pltpu.roll(here[0], TILE - 1, 1)
            up = jnp.concatenate(
                [jnp.where(is_first, side_up, tail)[None], here[: tiles - 1],
                 jnp.where(is_first, tail, side_up)[None]], 0)
            part = slice(g * SUB, (g + 1) * SUB)
            down = jnp.concatenate(
                [here[1:tiles],
                 (jnp.where(is_last, side_down, head) + source[part, :TILE])[None],
                 (jnp.where(is_last, head, side_down) + source[part, TILE:])[None]], 0)
            near = (prev + after) + (up + down)
            at = row_of(count, g)
            old[at] = (scale[at] * here - old[at]) + coef[at] * near
            prev, here = here, after
        for cb, values in interface(other, tiles - 1, TILE - 1):
            trace[cb, pl.ds(k, 1), :] = values

    def shell_step(k, cur, other):
        now, old, coef = planes.at[cur], planes.at[other], planes.at[2]
        terms = []
        for u in range(2):
            x = jnp.concatenate(
                [jnp.concatenate(
                    [now[u * half + t, pl.ds(pad + g, SUB, stride=groups), :]
                     for g in range(groups)], 0,
                ).astype(BF16) for t in range(half)], 1,
            )
            matrix = element[u]
            if u == 0:
                x = jnp.concatenate([x, wave_g[...]], 1)
                matrix = jnp.concatenate([matrix, picks[k]], 0)
            terms.append(jnp.dot(x, matrix, preferred_element_type=F32))

        def row(g):
            return [now[t, pl.ds(pad + g, SUB, stride=groups), :] for t in range(tiles)]

        prev, here = row(-1), row(0)
        for g in range(groups):
            after = row(g + 1)
            tails = [pltpu.roll(here[u * half + half - 1], 1, 1) for u in range(2)]
            heads = [pltpu.roll(here[u * half], TILE - 1, 1) for u in range(2)]
            for t in range(tiles):
                u, within = t // half, t % half
                if within:
                    up = here[t - 1]
                else:
                    up = jnp.where(is_first, tails[u - 1] if u else 0.0, tails[u])
                if within < half - 1:
                    down = here[t + 1]
                else:
                    down = jnp.where(is_last, 0.0 if u else heads[1], heads[u])
                term = terms[u][g * SUB : (g + 1) * SUB, within * TILE : (within + 1) * TILE]
                near = (prev[t] + after[t]) + (up + down) - term
                at = (t, pl.ds(pad + g, SUB, stride=groups), slice(None))
                old[at] = (scale[at] * here[t] - old[at]) + coef[at] * near
            prev, here = here, after
        for cb, values in interface(other, 0, 0):
            pieces[lax.div(k, deep), cb, pl.ds(lax.rem(k, deep), 1), :] = values

    def pair_of(step, between=None):
        def body(i, carry):
            if between is not None:

                @pl.when(i == deep // 2)
                def _():
                    between(0)

            step(2 * i, 0, 1)
            step(2 * i + 1, 1, 0)
            return carry

        lax.fori_loop(0, substeps // 2, body, 0)

    for ref in (planes.at[0], planes.at[1]):
        for t in range(tiles + 1):
            ref[t, pl.ds(0, pad), :] = jnp.zeros((pad, TILE), F32)
            ref[t, pl.ds(pad + wide, pad), :] = jnp.zeros((pad, TILE), F32)

    def hand_out(spacing):
        for a in range(2):
            for cb in range(blocks):
                for t in range(tiles):
                    block = planes[a, t, pl.ds(own + cb * TILE, TILE), :].T
                    for m in range(TILE // SUB):
                        fields_out[a, cb, spot(t, m, spacing), :] = block[
                            m * SUB : (m + 1) * SUB
                        ]

    @pl.when(on_shell)
    def _():
        def down(c, t):
            return remote(
                pieces.at[c], shell_pieces.at[c], down_send.at[c, t], down_recv.at[c], t, d
            )

        def send_piece(c):
            for t in range(shell):
                down(c, t).start()

        pair_of(shell_step, send_piece)
        send_piece(PIECES - 1)
        nodes_out[...] = jnp.zeros_like(nodes_out)
        hand_out(half)
        for t in range(shell):
            remote(total, parts.at[t], part_send, part_recv.at[t], t, d).wait_recv()
        sums = parts[0]
        for t in range(1, shell):
            sums = sums + parts[t]
        loads_out[...] = sums
        for c in range(PIECES):
            for t in range(shell):
                down(c, t).wait_send()

    @pl.when(on_fluid)
    def _():
        pair_of(fluid_step)
        terms = []
        for e in range(entries):
            x_high, x_low = split(trace[face[e]])
            first = jnp.dot(
                jnp.concatenate([x_high, x_low], 0), w_high[e], preferred_element_type=F32
            )
            second = jnp.dot(x_high, w_low[e], preferred_element_type=F32)
            terms.append(first[:SUB] + first[SUB:] + second)
        high, low = split(jnp.concatenate(terms, 0))
        halves = jnp.concatenate([high, low], 1)
        size = blocks * SUB
        for o in range(0, n_dom * size, TILE):
            result = jnp.dot(onehot[pl.ds(o, TILE), :], halves, preferred_element_type=F32)
            result = result[:, :TILE] + result[:, TILE:]
            for j in range(TILE // size):
                for b in range(blocks):
                    at = j * size + b * SUB
                    outgoing[o // size + j, b] = result[at : at + SUB]
        sends = []
        for j in range(1, n_dom):
            to = lax.rem(d + j, n_dom)
            copy = remote(
                outgoing.at[to], arrived.at[j - 1], load_send.at[j - 1], load_recv.at[j - 1],
                s, to,
            )
            copy.start()
            sends.append(copy)
        spread = []
        for c in range(PIECES):
            remote(
                pieces.at[c], shell_pieces.at[c], down_send.at[c, 0], down_recv.at[c], shell, d
            ).wait_recv()
            for j in range(1, n_dom):
                to = lax.rem(d + j, n_dom)
                copy = remote(
                    shell_pieces.at[c], nodes.at[j - 1, c], node_send.at[c, j - 1],
                    node_recv.at[c, j - 1], s, to,
                )
                copy.start()
                spread.append(copy)
        hand_out(tiles)
        value = outgoing[d]
        for j in range(1, n_dom):
            sends[j - 1].wait_recv()
            value = value + arrived[j - 1]
        total[...] = value
        pl.semaphore_wait(ready, 1)
        up = remote(total, parts.at[s], part_send, part_recv.at[s], shell, d)
        up.start()
        loads_out[...] = jnp.zeros_like(loads_out)
        for c in range(PIECES):
            rows_c = slice(deep * c, deep * (c + 1))
            nodes_out[0, :, rows_c, :] = shell_pieces[c]
            for j in range(1, n_dom):
                spread[c * (n_dom - 1) + j - 1].wait_recv()
                nodes_out[j, :, rows_c, :] = nodes[j - 1, c]
        for copy in sends + spread + [up]:
            copy.wait_send()


def window(
    face, owner, node, state, previous, coefficient, stiffness, wave, rbf, n_sect, n_dom
):
    rows, lanes = state.shape
    substeps = wave.shape[0]
    entries, size = rbf.shape[0], rbf.shape[1]
    tiles, blocks = rows // TILE, lanes // TILE
    wide = lanes + 2 * HALO
    deep = wide + 2 * SUB
    smem = pl.BlockSpec(memory_space=pltpu.SMEM)
    anywhere = pl.BlockSpec(memory_space=pltpu.HBM)
    vmem = pl.BlockSpec(memory_space=pltpu.VMEM)
    dma = pltpu.SemaphoreType.DMA
    block = (blocks, substeps, size)
    held = [
        pltpu.with_memory_space_constraint(x, pltpu.HBM)
        for x in (state, previous, coefficient, stiffness, wave, rbf)
    ]

    def full(*shape, dtype=F32):
        return pltpu.VMEM(shape, dtype)

    return pl.pallas_call(
        functools.partial(window_kernel, n_sect, n_dom),
        out_shape=(
            pltpu.VMEM((2, blocks, rows, TILE), F32),
            pltpu.VMEM(block, F32),
            pltpu.VMEM((n_dom,) + block, F32),
            pltpu.VMEM(rbf.shape, BF16),
            pltpu.VMEM(rbf.shape, BF16),
        ),
        in_specs=[smem] * 3 + [anywhere] * 6,
        out_specs=(vmem,) * 5,
        scratch_shapes=[
            full(4, blocks, rows, TILE),
            full(3, tiles + 1, deep, TILE),
            full(tiles + 1, deep, TILE),
            full(deep, TILE),
            full(wide, TILE, dtype=BF16),
            full(substeps, TILE, 2 * TILE, dtype=BF16),
            full(wide, 2 * TILE),
            full(4, blocks + 2, HALO, TILE),
            full(3, blocks + 2, HALO, TILE),
            full(blocks + 2, HALO, TILE),
            full(*rbf.shape),
            full(*wave.shape),
            full(n_dom * blocks * SUB, entries * SUB, dtype=BF16),
            full(*block),
            full(n_dom, *block),
            full(*stiffness.shape, dtype=BF16),
            full(2, rows // 2, rows // 2, dtype=BF16),
            full(tiles // 2, TILE, TILE),
            full(n_dom - 1, *block),
            full(*block),
            full(n_sect - 1, *block),
            full(n_dom - 1, PIECES, blocks, substeps // PIECES, size),
            full(PIECES, blocks, substeps // PIECES, size),
            full(PIECES, blocks, substeps // PIECES, size),
            dma((3 * blocks + 3,)),
            dma((10,)),
            dma((10,)),
            dma((n_dom - 1,)),
            dma((n_dom - 1,)),
            dma,
            dma((n_sect - 1,)),
            dma((PIECES, n_sect - 1)),
            dma((PIECES,)),
            dma((PIECES, n_dom - 1)),
            dma((PIECES, n_dom - 1)),
            pltpu.SemaphoreType.REGULAR,
        ],
        compiler_params=pltpu.CompilerParams(
            collective_id=0, has_side_effects=True, vmem_limit_bytes=59 * 1024 * 1024
        ),
        name="window",
    )(face, owner, node, *held)


def three_products(x, high, low):
    x_high, x_low = split(x)
    dims = (((1,), (1,)), ((), ()))
    both = jnp.concatenate([x_high, x_low], 0)
    first = lax.dot_general(both, high, dims, preferred_element_type=F32)
    second = lax.dot_general(x_high, low, dims, preferred_element_type=F32)
    return first[:SUB] + first[SUB:] + second


def pull_kernel(
    n_sect, n_dom, face, owner, node, fields, loads, nodes, w_high, w_low,
    state_out, previous_out, out, terms, sums, sems,
):
    entries = w_high.shape[0]
    substeps = out.shape[0]
    blocks = loads.shape[0]
    d = lax.axis_index("dom")
    on_shell = lax.axis_index("sect") == n_sect - 1
    leave = [
        pltpu.make_async_copy(
            fields.at[a, cb], target.at[:, pl.ds(cb * TILE, TILE)], sems.at[a * blocks + cb]
        )
        for a, target in enumerate((state_out, previous_out))
        for cb in range(blocks)
    ]
    for copy in leave:
        copy.start()

    @pl.when(on_shell)
    def _():
        for b in range(blocks):
            for k in range(substeps):
                out[k, :, b * TILE : (b + 1) * TILE] = loads[b, k : k + 1, :]

    @pl.when(jnp.logical_not(on_shell))
    def _():
        sums[...] = jnp.zeros_like(sums)
        for e in range(entries):
            slot = lax.rem(d - owner[e] + n_dom, n_dom)
            terms[e] = three_products(nodes[slot, node[e]], w_high[e], w_low[e])
        for e in range(entries):
            sums[face[e]] += terms[e]
        for b in range(blocks):
            for k in range(substeps):
                out[k, :, b * TILE : (b + 1) * TILE] = sums[b, k : k + 1, :]

    for copy in leave:
        copy.wait()


def pull(face, owner, node, fields, loads, nodes, w_high, w_low, n_sect, n_dom):
    _, blocks, rows, size = fields.shape
    substeps = loads.shape[1]
    lanes = blocks * size
    smem = pl.BlockSpec(memory_space=pltpu.SMEM)
    hbm = pl.BlockSpec(memory_space=pltpu.HBM)
    vmem = pl.BlockSpec(memory_space=pltpu.VMEM)
    held = [
        pltpu.with_memory_space_constraint(x, pltpu.VMEM)
        for x in (fields, loads, nodes, w_high, w_low)
    ]
    return pl.pallas_call(
        functools.partial(pull_kernel, n_sect, n_dom),
        out_shape=(
            jax.ShapeDtypeStruct((rows, lanes), F32),
            jax.ShapeDtypeStruct((rows, lanes), F32),
            jax.ShapeDtypeStruct((substeps, 1, lanes), F32),
        ),
        in_specs=[smem] * 3 + [vmem] * 5,
        out_specs=(hbm, hbm, vmem),
        scratch_shapes=[
            pltpu.VMEM((w_high.shape[0], substeps, size), F32),
            pltpu.VMEM((blocks, substeps, size), F32),
            pltpu.SemaphoreType.DMA((2 * blocks,)),
        ],
        compiler_params=pltpu.CompilerParams(vmem_limit_bytes=16 * 1024 * 1024),
        name="pull",
    )(face, owner, node, *held)


def local(
    state, previous, coefficient, stiffness, waveform, entry_face, entry_owner, entry_node, rbf
):
    n_sect = lax.axis_size("sect")
    n_dom = lax.axis_size("dom")
    owner = entry_owner.reshape(entry_owner.shape[0])
    fields, loads, nodes, w_high, w_low = window(
        entry_face, owner, entry_node, state, previous, coefficient, stiffness, waveform, rbf,
        n_sect, n_dom,
    )
    return pull(
        entry_face, owner, entry_node, fields, loads, nodes, w_high, w_low, n_sect, n_dom
    )


def solution(mesh):
    in_specs = (
        P("sect", "dom"),
        P("sect", "dom"),
        P("sect", "dom"),
        P(),
        P(None, ("sect", "dom"), None),
        P(("sect", "dom")),
        P(("sect", "dom"), None),
        P(("sect", "dom")),
        P(("sect", "dom"), None, None),
    )
    out_specs = (P("sect", "dom"), P("sect", "dom"), P(None, ("sect", "dom"), None))
    return jax.shard_map(local, mesh=mesh, in_specs=in_specs, out_specs=out_specs, check_vma=False)
```
